256 devices in a mesh: row: 16 (over z, core), col: 16 (over x, y).
Axes of the slice: x: 4, y: 4, z: 8, core: 2. Of those that a mesh axis runs over, the one named last changes fastest.
Arguments:
- tile_values: float32 [12288, 32, 1024], P(('row', 'col')), may hold values from -6 to 6
- tile_count: int32 [256], P(('row', 'col')), may hold values from 1 to 48, as said below
- mode1_column: int32 [12288, 1], P(('row', 'col')), may hold values from 0 to 15; in each aligned block of 48 rows (0 to 47, 48 to 95, ...) at most 4 rows name the same one
- mode1_offset: int32 [12288], P(('row', 'col')), may hold values from 0 to 15
- mode2_row: int32 [12288, 1], P(('row', 'col')), may hold values from 0 to 15; in each aligned block of 48 rows (0 to 47, 48 to 95, ...) at most 4 rows name the same one
- mode2_offset: int32 [12288], P(('row', 'col')), may hold values from 0 to 7
- mode3_offset: int32 [12288], P(('row', 'col')), may hold values from 0 to 15
- mode2_factor: float32 [65536, 256], P(('row', 'col'))
- mode3_factor: float32 [8192, 256], P('col')
Outputs:
- updated: float32 [131072, 256], P(('row', 'col'))
The draws below stay inside these ranges and needn't reach their ends.
Inputs may be any that keep to these rules, and one draw needn't show every extreme that they name: Device d's live tiles fill its first tile_count[d] slots; other slots are ignored. Some device holds 48 live tiles. `mode1_column`: at most 4 slots of one device name the same value, and some device reaches it. `mode2_row`: at most 4 slots of one device name the same value, and some device reaches it.
All inputs are finite; a program needn't handle non-finite values.
Results may differ from the reference program's by a relative error of at most 0.0003.
Values sent between devices are 32-bit elements; how exact they have to be, the bound alone decides.
No kernel may reach another device: no remote copies, remote signals or barrier semaphores. Data moves between devices by JAX's collectives and lax.ppermute only.
A program may use at most 128 MiB of HBM per device.

```python
import math
import jax
import jax.numpy as jnp
import numpy as np
from jax import lax

RANK = 256
TILE = 32
TILES_DEV = 48
IB_DEV = 16
JB_DEV = 8
KB_COL = 16
TILES = 12288
I = 131072
J = 65536
K = 8192
ACAP = 4
BCAP = 4
N_ROW = 16
N_COL = 16
DEVICES = 256


def draw_tile_count(key, part):
    spread_key, busy_key = jax.random.split(jax.random.fold_in(key, 3))
    span_width = max(1, TILES_DEV // 4)
    floor_count = TILES_DEV - span_width
    drawn_values = jax.random.randint(spread_key, (DEVICES,), 0, span_width + 1)
    counts = floor_count + (drawn_values * drawn_values + span_width - 1) // span_width
    busiest = jax.random.randint(busy_key, (), 0, DEVICES)
    return jnp.where(jnp.arange(DEVICES) == busiest, TILES_DEV, counts).astype(jnp.int32)


def draw_factor(key, row_total, salt_value):
    key_list = jax.random.split(jax.random.fold_in(key, salt_value), 4)
    position = jnp.arange(row_total, dtype=jnp.float32)[:, None] / row_total
    rough_scale = jnp.exp(jax.random.uniform(key_list[0], (row_total, 1), jnp.float32, -1.15, 1.15))
    column_scale = jnp.exp(jax.random.uniform(key_list[1], (1, RANK), jnp.float32, 0.0, 1.1))
    shared = jnp.clip(jax.random.normal(key_list[2], (row_total, 1), jnp.float32), -4.0, 4.0)
    ramp_scale = 0.6 + 1.2 * position
    noise_part = jnp.clip(jax.random.normal(key_list[3], (row_total, RANK), jnp.float32), -5.0, 5.0)
    shared_weight = 0.6
    return ramp_scale * rough_scale * column_scale * (noise_part + shared_weight * shared) * (0.5 * math.sqrt(TILE) / row_total)


def draw_mode2_factor(key, part):
    return draw_factor(key, J, 21)


def draw_mode3_factor(key, part):
    return draw_factor(key, K, 22)


def touch_ends(values, own_key, low, top_value):
    place = [jax.random.randint(jax.random.fold_in(own_key, axis), (), 0, length) for axis, length in enumerate(values.shape)]
    longest = values.shape.index(max(values.shape))
    next_to = place[:longest] + [(place[longest] + 1) % values.shape[longest]] + place[longest + 1:]
    return values.at[tuple(place)].set(low).at[tuple(next_to)].set(top_value)


def shard_levels(own_key, dims, cuts, least, high):
    level = 1.0
    for axis_at, parts in cuts:
        steps = jax.random.uniform(jax.random.fold_in(jax.random.fold_in(own_key, 6), axis_at), (parts,), jnp.float32, least / len(cuts), high / len(cuts))
        level = level * jnp.repeat(jnp.exp(steps), dims[axis_at] // parts).reshape((-1,) + (1,) * (len(dims) - 1 - axis_at))
    return level


def assign_block(stream_key, own, number, rows, number_of, top, limit, slope):
    ranking = jax.random.permutation(stream_key, number_of)
    packed, common = load_shares(number_of, rows * top, limit, slope, True), load_shares(number_of, rows * top, limit, slope, False)
    places = jnp.arange(number_of)

    def named(lengths, turn):
        used = int((lengths > 0).sum())
        fixed = max(1, used // 4)
        moved = fixed + (places - fixed + turn * (used - fixed)) % max(1, number_of - fixed)
        return jnp.zeros((number_of,), jnp.int32).at[ranking[jnp.where(places < fixed, places, moved)]].set(jnp.asarray(lengths, jnp.int32))

    lengths = jnp.where(number % 4 == 0, named(packed, number // 4), named(common, number - number // 4 - 1))
    mixed = jax.random.permutation(jax.random.fold_in(own, 3), number_of)
    giver, receiver = mixed[0:number_of // 2 * 2:2], mixed[1:number_of // 2 * 2:2]
    margin = jnp.minimum(lengths[giver] - 1, limit - lengths[receiver]) // 2
    margin = jnp.where((giver == ranking[0]) | (receiver == ranking[0]) | (lengths[receiver] == 0), 0, jnp.maximum(margin, 0))
    moved = jax.random.randint(jax.random.fold_in(own, 4), (number_of // 2,), 0, 1 << 20) % (margin + 1)
    lengths = lengths.at[giver].add(-moved).at[receiver].add(moved)
    labels = jnp.searchsorted(jnp.cumsum(lengths), jnp.arange(rows * top), side="right").astype(jnp.int32)
    table = labels.reshape(top, rows).T
    table = table[jax.random.permutation(jax.random.fold_in(own, 1), rows)]
    turn = jax.random.randint(jax.random.fold_in(own, 2), (rows, 1), 0, top)
    return jnp.take_along_axis(table, (jnp.arange(top)[None, :] + turn) % top, axis=1)


def load_shares(count, total, reach, slope, full):
    weights = [(1 << 20) // math.isqrt(grade ** slope) + 1 for grade in range(1, count + 1)]
    largest = reach if full else min(reach, max(-(-total // count), total * weights[0] // sum(weights)))
    least = 1 if total - largest >= count - 1 else 0
    holding, surplus = [largest] + [least] * (count - 1), total - largest - least * (count - 1)
    while surplus > 0:
        free = [i for i in range(1, count) if holding[i] < largest] or [i for i in range(1, count) if holding[i] < reach]
        whole, left = sum([weights[i] for i in free]), surplus
        for i in free:
            addition = min(reach - holding[i], max(1, left * weights[i] // whole), surplus)
            holding[i] = holding[i] + addition
            surplus = surplus - addition
    return np.array(holding)


def normal_values(rng, extent, width, most, cuts=(), held_as=jnp.bfloat16):
    entries = jax.random.normal(rng, extent, jnp.float32) * width
    if len(cuts) > 0:
        entries = shard_levels(rng, extent, cuts, -0.22, 0.18) * entries
    return jnp.clip(entries, min=-most, max=most).astype(held_as)


def setup_inputs(seed: int = 0) -> dict:
    key_of = jax.random.split(jax.random.key(seed), 10)
    tile_values = normal_values(key_of[0], (TILES, TILE, TILE * TILE), 1.0, 6.0, ((0, 256),), jnp.float32)
    tile_count = draw_tile_count(jax.random.fold_in(key_of[9], 71), 0)
    mode1_column_keys = jax.random.split(jax.random.fold_in(key_of[2], 1), TILES // TILES_DEV)
    mode1_column_turns = jax.random.permutation(jax.random.fold_in(key_of[2], 3), TILES // TILES_DEV)
    mode1_column = jax.vmap(lambda own, number: assign_block(jax.random.fold_in(key_of[2], 2), own, number, TILES_DEV, N_COL, 1, ACAP, 2))(mode1_column_keys, mode1_column_turns).reshape((TILES, 1))
    mode1_offset = touch_ends(jax.random.randint(key_of[3], (TILES,), 0, IB_DEV), jax.random.fold_in(key_of[3], 1), 0, IB_DEV - 1).astype(jnp.int32)
    mode2_row_keys = jax.random.split(jax.random.fold_in(key_of[4], 1), TILES // TILES_DEV)
    mode2_row_turns = jax.random.permutation(jax.random.fold_in(key_of[4], 3), TILES // TILES_DEV)
    mode2_row = jax.vmap(lambda own, number: assign_block(jax.random.fold_in(key_of[4], 2), own, number, TILES_DEV, N_ROW, 1, BCAP, 2))(mode2_row_keys, mode2_row_turns).reshape((TILES, 1))
    mode2_offset = touch_ends(jax.random.randint(key_of[5], (TILES,), 0, JB_DEV), jax.random.fold_in(key_of[5], 1), 0, JB_DEV - 1).astype(jnp.int32)
    mode3_offset = touch_ends(jax.random.randint(key_of[6], (TILES,), 0, KB_COL), jax.random.fold_in(key_of[6], 1), 0, KB_COL - 1).astype(jnp.int32)
    mode2_factor = draw_mode2_factor(jax.random.fold_in(key_of[9], 71), 0)
    mode3_factor = draw_mode3_factor(jax.random.fold_in(key_of[9], 71), 0)
    return {"tile_values": tile_values, "tile_count": tile_count, "mode1_column": mode1_column, "mode1_offset": mode1_offset, "mode2_row": mode2_row, "mode2_offset": mode2_offset, "mode3_offset": mode3_offset, "mode2_factor": mode2_factor, "mode3_factor": mode3_factor}


HIGHEST_PRECISION = lax.Precision.HIGHEST

def product_of(left_matrix, right_matrix):
    return lax.dot_general(left_matrix.astype(jnp.float32), right_matrix.astype(jnp.float32), (((0,), (0,)), ((), ())), precision=HIGHEST_PRECISION, preferred_element_type=jnp.float32)

def reference(tile_values, tile_count, mode1_column, mode1_offset, mode2_row, mode2_offset, mode3_offset, mode2_factor, mode3_factor):
    tile_total = tile_values.shape[0]
    tile_edge = tile_values.shape[1]
    rank_width = mode2_factor.shape[1]
    slot_index = jnp.arange(tile_total, dtype=jnp.int32)
    device_index = slot_index // TILES_DEV
    grid_row = device_index // N_COL
    grid_column = device_index % N_COL
    is_live = slot_index % TILES_DEV < tile_count[device_index]
    mode1_block = ((grid_row * N_COL + mode1_column[:, 0]) * IB_DEV + mode1_offset).astype(jnp.int32)
    mode2_block = ((mode2_row[:, 0] * N_COL + grid_column) * JB_DEV + mode2_offset).astype(jnp.int32)
    mode3_block = (grid_column * KB_COL + mode3_offset).astype(jnp.int32)

    def contribute(slot_at, carried):
        second_rows = lax.dynamic_slice_in_dim(mode2_factor, (mode2_block[slot_at] * tile_edge).astype(jnp.int32), tile_edge, 0)
        third_rows = lax.dynamic_slice_in_dim(mode3_factor, (mode3_block[slot_at] * tile_edge).astype(jnp.int32), tile_edge, 0)
        khatri = (second_rows[:, None, :] * third_rows[None, :, :]).reshape(tile_edge * tile_edge, rank_width)
        product_rows = jnp.dot(tile_values[slot_at].astype(jnp.float32), khatri.astype(jnp.float32), precision=HIGHEST_PRECISION, preferred_element_type=jnp.float32)
        row_start = (mode1_block[slot_at] * tile_edge).astype(jnp.int32)
        current_rows = lax.dynamic_slice_in_dim(carried, row_start, tile_edge, 0)
        return lax.dynamic_update_slice_in_dim(carried, current_rows + product_rows, row_start, 0)

    def visit_slot(slot_at, carried):
        return lax.cond(is_live[slot_at], lambda inner: contribute(slot_at, inner), lambda inner: inner, carried)
    mttkrp = lax.fori_loop(0, tile_total, visit_slot, jnp.zeros((I, rank_width), jnp.float32))
    normal_matrix = product_of(mode2_factor, mode2_factor) * product_of(mode3_factor, mode3_factor)
    cholesky_factor = jnp.linalg.cholesky(normal_matrix)
    return jax.scipy.linalg.cho_solve((cholesky_factor, True), mttkrp.T).T
```

```python
import jax
import jax.numpy as jnp
from jax import lax
from jax.experimental import pallas as pl
from jax.experimental.pallas import tpu as pltpu
from jax.sharding import PartitionSpec as P

IB_DEV = 16
JB_DEV = 8
SLOTS = 4
PAIR = 2

HIGHEST = lax.Precision.HIGHEST


def gram_of(matrix):
    return lax.dot_general(
        matrix, matrix, (((0,), (0,)), ((), ())), precision=HIGHEST, preferred_element_type=jnp.float32
    )


def split(value):
    high = value.astype(jnp.bfloat16)
    low = (value - high.astype(jnp.float32)).astype(jnp.bfloat16)
    return high, low


def dot32(left, right):
    return jnp.dot(left, right, preferred_element_type=jnp.float32)


def contract_kernel(
    table_ref, count_ref, tile_hbm, second_hbm, third_ref, out_ref, tile_buf, second_buf, tile_sem, second_sem
):
    count = count_ref[0]
    pairs = (count + PAIR - 1) // PAIR
    tile_edge = third_ref.shape[1]
    depth = tile_buf.shape[2]
    chunk = min(256, depth)
    per_chunk = chunk // tile_edge

    def tile_copy(pair):
        return pltpu.make_async_copy(
            tile_hbm.at[pl.ds(pair * PAIR, PAIR)], tile_buf.at[pl.ds(pair * PAIR, PAIR)], tile_sem.at[pair]
        )

    def second_copy(slot):
        return pltpu.make_async_copy(
            second_hbm.at[table_ref[0, slot]], second_buf.at[slot], second_sem.at[slot]
        )

    def start(pair, carry):
        tile_copy(pair).start()
        for at in range(PAIR):
            second_copy(pair * PAIR + at).start()
        return carry

    lax.fori_loop(0, pairs, start, 0)
    out_ref[...] = jnp.zeros_like(out_ref)

    def contract(pair, carry):
        tile_copy(pair).wait()
        for at in range(PAIR):
            second_copy(pair * PAIR + at).wait()
        for at in range(PAIR):
            slot = pair * PAIR + at
            second = second_buf[slot]
            third = third_ref[table_ref[1, slot]]
            high, low = split(tile_buf[slot])
            both = jnp.concatenate([high, low], axis=0)
            total = jnp.zeros((2 * tile_edge, third.shape[1]), jnp.float32)
            total_low = jnp.zeros((tile_edge, third.shape[1]), jnp.float32)
            for q in range(depth // chunk):
                rows = second[q * per_chunk : (q + 1) * per_chunk]
                khatri = (rows[:, None, :] * third[None, :, :]).reshape(chunk, third.shape[1])
                khatri_high, khatri_low = split(khatri)
                total = total + dot32(both[:, q * chunk : (q + 1) * chunk], khatri_high)
                total_low = total_low + dot32(high[:, q * chunk : (q + 1) * chunk], khatri_low)
            result = total[:tile_edge] + (total[tile_edge:] + total_low)

            @pl.when(slot < count)
            def _():
                out_ref[table_ref[2, slot]] = result

        return carry

    lax.fori_loop(0, pairs, contract, 0)


def contract_tiles(table, count, tile_values, second_blocks, third_blocks, out_slots):
    slot_count, tile_edge, depth = tile_values.shape
    rank_width = third_blocks.shape[2]
    smem = pl.BlockSpec(memory_space=pltpu.SMEM)
    vmem = pl.BlockSpec(memory_space=pltpu.VMEM)
    hbm = pl.BlockSpec(memory_space=pl.ANY)
    return pl.pallas_call(
        contract_kernel,
        out_shape=jax.ShapeDtypeStruct((out_slots, tile_edge, rank_width), jnp.float32),
        in_specs=[smem, smem, hbm, hbm, vmem],
        out_specs=vmem,
        scratch_shapes=[
            pltpu.VMEM((slot_count, tile_edge, depth), jnp.float32),
            pltpu.VMEM((slot_count, tile_edge, rank_width), jnp.float32),
            pltpu.SemaphoreType.DMA((slot_count // PAIR,)),
            pltpu.SemaphoreType.DMA((slot_count,)),
        ],
        compiler_params=pltpu.CompilerParams(vmem_limit_bytes=28 * 1024 * 1024),
        cost_estimate=pl.CostEstimate(
            flops=6 * slot_count * tile_edge * depth * rank_width, bytes_accessed=10_000_000, transcendentals=0
        ),
        name="contract",
    )(table, count, tile_values, second_blocks, third_blocks)


def combine_kernel(target_ref, received_ref, inverse_ref, out_ref, total_ref):
    tile_edge = received_ref.shape[1]
    total_ref[...] = jnp.zeros_like(total_ref)

    def add(slot, carry):
        target = target_ref[slot]

        @pl.when(target >= 0)
        def _():
            rows = pl.ds(pl.multiple_of(target * tile_edge, tile_edge), tile_edge)
            total_ref[rows, :] += received_ref[slot]

        return carry

    lax.fori_loop(0, received_ref.shape[0], add, 0)
    out_ref[...] = jnp.dot(
        total_ref[...], inverse_ref[...], precision=HIGHEST, preferred_element_type=jnp.float32
    )


def combine(targets, received, inverse):
    tile_edge, rank_width = received.shape[1:]
    vmem = pl.BlockSpec(memory_space=pltpu.VMEM)
    return pl.pallas_call(
        combine_kernel,
        out_shape=jax.ShapeDtypeStruct((IB_DEV * tile_edge, rank_width), jnp.float32),
        in_specs=[pl.BlockSpec(memory_space=pltpu.SMEM), vmem, vmem],
        out_specs=vmem,
        scratch_shapes=[pltpu.VMEM((IB_DEV * tile_edge, rank_width), jnp.float32)],
        compiler_params=pltpu.CompilerParams(vmem_limit_bytes=16 * 1024 * 1024),
        name="combine",
    )(targets, received, inverse)


def local(
    tile_values,
    tile_count,
    mode1_column,
    mode1_offset,
    mode2_row,
    mode2_offset,
    mode3_offset,
    mode2_factor,
    mode3_factor,
):
    slot_count, tile_edge, _ = tile_values.shape
    rank_width = mode2_factor.shape[1]
    row_index = lax.axis_index("row")
    col_index = lax.axis_index("col")
    n_row = lax.axis_size("row")
    n_col = lax.axis_size("col")
    part = rank_width // n_row

    with jax.named_scope("gather_second"):
        gathered = lax.all_gather(mode2_factor, "row", axis=0, tiled=True)

    with jax.named_scope("tables"):
        slot_index = jnp.arange(slot_count, dtype=jnp.int32)
        is_live = slot_index < tile_count[0]
        chosen = (mode1_column[:, 0][None, :] == jnp.arange(n_col, dtype=jnp.int32)[:, None]) & is_live[None, :]
        chosen = chosen.astype(jnp.float32)
        earlier = (slot_index[:, None] < slot_index[None, :]).astype(jnp.float32)
        rank = jnp.dot(chosen, earlier)
        own_rank = jnp.sum(chosen * rank, axis=0).astype(jnp.int32)
        out_slot = jnp.clip(mode1_column[:, 0], 0, n_col - 1) * SLOTS + own_rank
        table = jnp.stack(
            [
                jnp.clip(mode2_row[:, 0] * JB_DEV + mode2_offset, 0, gathered.shape[0] // tile_edge - 1),
                jnp.clip(mode3_offset, 0, mode3_factor.shape[0] // tile_edge - 1),
                out_slot,
            ]
        ).astype(jnp.int32)
        place = jnp.arange(SLOTS, dtype=jnp.float32)
        taken = chosen[:, None, :] * (rank[:, None, :] == place[None, :, None])
        targets = jnp.sum(taken * (mode1_offset + 1).astype(jnp.float32), axis=2) - 1.0
        target_rows = jnp.zeros((8, rank_width), jnp.float32).at[0, : n_col * SLOTS].set(targets.reshape(-1))

    with jax.named_scope("normal"):
        own_second = gram_of(mode2_factor)
        own_third = gram_of(mode3_factor)
        exchanged = lax.all_to_all(own_second.reshape(n_row, part, rank_width), "row", 0, 0)
        second_part = jnp.sum(exchanged, axis=0)
        third_part = lax.dynamic_slice_in_dim(own_third, row_index * part, part, 0)
        sent = jnp.concatenate([second_part, third_part, target_rows], axis=0)
        spread = lax.all_gather(sent, "col", axis=0)
        both = jnp.sum(spread[:, : 2 * part], axis=0)
        normal_part = both[:part] * both[part:]
        normal_matrix = lax.all_gather(normal_part, "row", axis=0, tiled=True)
        received_targets = lax.dynamic_slice_in_dim(spread[:, 2 * part], col_index * SLOTS, SLOTS, 1)
        received_targets = received_targets.astype(jnp.int32).reshape(-1)

    with jax.named_scope("contract"):
        partials = contract_tiles(
            table,
            tile_count,
            tile_values,
            gathered.reshape(-1, tile_edge, rank_width),
            mode3_factor.reshape(-1, tile_edge, rank_width),
            n_col * SLOTS,
        )
    with jax.named_scope("exchange"):
        received = lax.all_to_all(
            partials.reshape(n_col, SLOTS * tile_edge, rank_width), "col", 0, 0
        ).reshape(n_col * SLOTS, tile_edge, rank_width)

    with jax.named_scope("inverse"):
        factor = jnp.linalg.cholesky(normal_matrix)
        inverse = jax.scipy.linalg.cho_solve((factor, True), jnp.eye(rank_width, dtype=jnp.float32))

    with jax.named_scope("combine"):
        return combine(received_targets, received, inverse)


def solution(mesh):
    placed = (
        P(("row", "col"), None, None),
        P(("row", "col")),
        P(("row", "col"), None),
        P(("row", "col")),
        P(("row", "col"), None),
        P(("row", "col")),
        P(("row", "col")),
        P(("row", "col"), None),
        P("col", None),
    )
    return jax.shard_map(
        local, mesh=mesh, in_specs=placed, out_specs=P(("row", "col"), None), check_vma=False
    )
```

```python
import functools

import jax
import jax.numpy as jnp
from jax import lax
from jax.experimental import pallas as pl
from jax.experimental.pallas import tpu as pltpu
from jax.sharding import PartitionSpec as P

IB_DEV = 16
JB_DEV = 8
SLOTS = 4
PAIR = 2

HIGHEST = lax.Precision.HIGHEST


def gram_of(matrix):
    return lax.dot_general(
        matrix, matrix, (((0,), (0,)), ((), ())), precision=HIGHEST, preferred_element_type=jnp.float32
    )


def split(value):
    high = value.astype(jnp.bfloat16)
    low = (value - high.astype(jnp.float32)).astype(jnp.bfloat16)
    return high, low


def dot32(left, right):
    return jnp.dot(left, right, preferred_element_type=jnp.float32)


def contract_kernel(
    table_ref,
    count_ref,
    tile_hbm,
    second_hbm,
    third_ref,
    out_hbm,
    tile_buf,
    second_buf,
    result_buf,
    tile_sem,
    second_sem,
    result_sem,
):
    count = count_ref[0]
    pairs = (count + PAIR - 1) // PAIR
    tile_edge = third_ref.shape[1]
    depth = tile_buf.shape[2]
    chunk = min(256, depth)
    per_chunk = chunk // tile_edge

    def tile_copy(pair):
        return pltpu.make_async_copy(
            tile_hbm.at[pl.ds(pair * PAIR, PAIR)], tile_buf.at[pl.ds(pair * PAIR, PAIR)], tile_sem.at[pair]
        )

    def second_copy(slot):
        return pltpu.make_async_copy(
            second_hbm.at[table_ref[0, slot]], second_buf.at[slot], second_sem.at[slot]
        )

    def result_copy(slot):
        return pltpu.make_async_copy(result_buf.at[slot], out_hbm.at[table_ref[2, slot]], result_sem.at[slot])

    def start(pair, carry):
        tile_copy(pair).start()
        for at in range(PAIR):
            second_copy(pair * PAIR + at).start()
        return carry

    lax.fori_loop(0, pairs, start, 0)

    def contract(pair, carry):
        tile_copy(pair).wait()
        for at in range(PAIR):
            second_copy(pair * PAIR + at).wait()
        for at in range(PAIR):
            slot = pair * PAIR + at
            second = second_buf[slot]
            third = third_ref[table_ref[1, slot]]
            high, low = split(tile_buf[slot])
            both = jnp.concatenate([high, low], axis=0)
            total = jnp.zeros((2 * tile_edge, third.shape[1]), jnp.float32)
            total_low = jnp.zeros((tile_edge, third.shape[1]), jnp.float32)
            for q in range(depth // chunk):
                rows = second[q * per_chunk : (q + 1) * per_chunk]
                khatri = (rows[:, None, :] * third[None, :, :]).reshape(chunk, third.shape[1])
                khatri_high, khatri_low = split(khatri)
                total = total + dot32(both[:, q * chunk : (q + 1) * chunk], khatri_high)
                total_low = total_low + dot32(high[:, q * chunk : (q + 1) * chunk], khatri_low)
            result_buf[slot] = total[:tile_edge] + (total[tile_edge:] + total_low)

            @pl.when(slot < count)
            def _():
                result_copy(slot).start()

        return carry

    lax.fori_loop(0, pairs, contract, 0)

    def finish(slot, carry):
        result_copy(slot).wait()
        return carry

    lax.fori_loop(0, count, finish, 0)


def contract_tiles(table, count, tile_values, second_blocks, third_blocks, out_slots):
    slot_count, tile_edge, depth = tile_values.shape
    rank_width = third_blocks.shape[2]
    smem = pl.BlockSpec(memory_space=pltpu.SMEM)
    vmem = pl.BlockSpec(memory_space=pltpu.VMEM)
    hbm = pl.BlockSpec(memory_space=pltpu.HBM)
    return pl.pallas_call(
        contract_kernel,
        out_shape=jax.ShapeDtypeStruct((out_slots, tile_edge, rank_width), jnp.float32),
        in_specs=[smem, smem, hbm, hbm, vmem],
        out_specs=hbm,
        scratch_shapes=[
            pltpu.VMEM((slot_count, tile_edge, depth), jnp.float32),
            pltpu.VMEM((slot_count, tile_edge, rank_width), jnp.float32),
            pltpu.VMEM((slot_count, tile_edge, rank_width), jnp.float32),
            pltpu.SemaphoreType.DMA((slot_count // PAIR,)),
            pltpu.SemaphoreType.DMA((slot_count,)),
            pltpu.SemaphoreType.DMA((slot_count,)),
        ],
        compiler_params=pltpu.CompilerParams(vmem_limit_bytes=60 * 1024 * 1024),
        cost_estimate=pl.CostEstimate(
            flops=6 * slot_count * tile_edge * depth * rank_width, bytes_accessed=10_000_000, transcendentals=0
        ),
        name="contract",
    )(table, count, tile_values, second_blocks, third_blocks)


def combine_kernel(target_ref, received_ref, inverse_ref, out_ref, total_ref):
    tile_edge = received_ref.shape[1]
    total_ref[...] = jnp.zeros_like(total_ref)

    def add(slot, carry):
        target = target_ref[slot]

        @pl.when(target >= 0)
        def _():
            rows = pl.ds(pl.multiple_of(target * tile_edge, tile_edge), tile_edge)
            total_ref[rows, :] += received_ref[slot]

        return carry

    lax.fori_loop(0, received_ref.shape[0], add, 0)
    out_ref[...] = jnp.dot(
        total_ref[...], inverse_ref[...], precision=HIGHEST, preferred_element_type=jnp.float32
    )


def combine(targets, received, inverse):
    tile_edge, rank_width = received.shape[1:]
    vmem = pl.BlockSpec(memory_space=pltpu.VMEM)
    return pl.pallas_call(
        combine_kernel,
        out_shape=jax.ShapeDtypeStruct((IB_DEV * tile_edge, rank_width), jnp.float32),
        in_specs=[pl.BlockSpec(memory_space=pltpu.SMEM), vmem, vmem],
        out_specs=vmem,
        scratch_shapes=[pltpu.VMEM((IB_DEV * tile_edge, rank_width), jnp.float32)],
        compiler_params=pltpu.CompilerParams(vmem_limit_bytes=16 * 1024 * 1024),
        name="combine",
    )(targets, received, inverse)


def invert_four(s):
    det = s[0][0] * s[1][1] - s[0][1] * s[0][1]
    over = 1.0 / det
    a00, a01, a11 = s[1][1] * over, -s[0][1] * over, s[0][0] * over
    y00 = a00 * s[0][2] + a01 * s[1][2]
    y01 = a00 * s[0][3] + a01 * s[1][3]
    y10 = a01 * s[0][2] + a11 * s[1][2]
    y11 = a01 * s[0][3] + a11 * s[1][3]
    c00 = s[2][2] - (s[0][2] * y00 + s[1][2] * y10)
    c01 = s[2][3] - (s[0][2] * y01 + s[1][2] * y11)
    c11 = s[3][3] - (s[0][3] * y01 + s[1][3] * y11)
    over = 1.0 / (c00 * c11 - c01 * c01)
    d00, d01, d11 = c11 * over, -c01 * over, c00 * over
    e00 = -(y00 * d00 + y01 * d01)
    e01 = -(y00 * d01 + y01 * d11)
    e10 = -(y10 * d00 + y11 * d01)
    e11 = -(y10 * d01 + y11 * d11)
    b00 = a00 - (e00 * y00 + e01 * y01)
    b01 = a01 - (e00 * y10 + e01 * y11)
    b11 = a11 - (e10 * y10 + e11 * y11)
    return [[b00, b01, e00, e01], [b01, b11, e10, e11], [e00, e10, d00, d01], [e01, e11, d01, d11]]

def invert_block(groups):
    width = groups[0].shape[1]
    full = (8, width)
    lane = lax.broadcasted_iota(jnp.int32, full, 1)
    sub = lax.broadcasted_iota(jnp.int32, full, 0)
    for first in range(0, width, 4):
        at, off = first // 8, first % 8
        cols = [[jnp.broadcast_to(g[:, first + j : first + j + 1], full) for j in range(4)] for g in groups]
        s = [[jnp.broadcast_to(cols[at][j][off + i : off + i + 1], full) if i <= j else None for j in range(4)] for i in range(4)]
        rows = [jnp.broadcast_to(groups[at][off + i : off + i + 1], full) for i in range(4)]
        d = invert_four(s)
        new_rows = []
        for i in range(4):
            w = d[i][0] * rows[0] + d[i][1] * rows[1] + d[i][2] * rows[2] + d[i][3] * rows[3]
            for j in range(4):
                w = jnp.where(lane == first + j, d[i][j], w)
            new_rows.append(w)
        in_pivot = (lane >= first) & (lane < first + 4)
        out = []
        for k, g in enumerate(groups):
            v = jnp.where(in_pivot, 0.0, g)
            v = v - ((cols[k][0] * new_rows[0] + cols[k][1] * new_rows[1]) + (cols[k][2] * new_rows[2] + cols[k][3] * new_rows[3]))
            if k == at:
                for i in range(4):
                    v = jnp.where(sub == off + i, new_rows[i], v)
            out.append(v)
        groups = out
    return groups

def invert_kernel(block, normal_ref, out_ref, work_ref):
    n = normal_ref.shape[0]
    normal = normal_ref[...]
    on_diagonal = lax.broadcasted_iota(jnp.int32, (n, n), 0) == lax.broadcasted_iota(jnp.int32, (n, n), 1)
    diagonal = jnp.where(on_diagonal, normal, 0.0)
    scale_row = lax.rsqrt(jnp.sum(diagonal, axis=0, keepdims=True))
    scale_col = lax.rsqrt(jnp.sum(diagonal, axis=1, keepdims=True))
    work_ref[...] = normal * scale_col * scale_row
    for first in range(0, n, block):
        last = first + block
        groups = [work_ref[r : r + 8, first:last] for r in range(first, last, 8)]
        inner = jnp.concatenate(invert_block(groups), axis=0)
        rows = jnp.dot(inner, work_ref[first:last, :], precision=HIGHEST, preferred_element_type=jnp.float32)
        pieces = [rows[:, :first]] if first else []
        pieces.append(inner)
        if last < n:
            pieces.append(rows[:, last:])
        rows = jnp.concatenate(pieces, axis=1)
        change = jnp.dot(work_ref[:, first:last], rows, precision=HIGHEST, preferred_element_type=jnp.float32)
        lane = lax.broadcasted_iota(jnp.int32, (n, n), 1)
        work_ref[...] = jnp.where((lane >= first) & (lane < last), 0.0, work_ref[...]) - change
        work_ref[first:last, :] = rows
    out_ref[...] = work_ref[...] * scale_col * scale_row

def invert(normal, block=64):
    n = normal.shape[0]
    vmem = pl.BlockSpec(memory_space=pltpu.VMEM)
    return pl.pallas_call(
        functools.partial(invert_kernel, block),
        out_shape=jax.ShapeDtypeStruct((n, n), jnp.float32),
        in_specs=[vmem], out_specs=vmem,
        scratch_shapes=[pltpu.VMEM((n, n), jnp.float32)],
        compiler_params=pltpu.CompilerParams(vmem_limit_bytes=16 * 1024 * 1024),
        cost_estimate=pl.CostEstimate(flops=12 * n * n * n, bytes_accessed=8 * n * n, transcendentals=0),
        name="invert",
    )(normal)


def local(
    tile_values,
    tile_count,
    mode1_column,
    mode1_offset,
    mode2_row,
    mode2_offset,
    mode3_offset,
    mode2_factor,
    mode3_factor,
):
    slot_count, tile_edge, _ = tile_values.shape
    rank_width = mode2_factor.shape[1]
    row_index = lax.axis_index("row")
    col_index = lax.axis_index("col")
    n_row = lax.axis_size("row")
    n_col = lax.axis_size("col")
    part = rank_width // n_row

    with jax.named_scope("gather_second"):
        gathered = lax.all_gather(mode2_factor, "row", axis=0, tiled=True)

    with jax.named_scope("tables"):
        slot_index = jnp.arange(slot_count, dtype=jnp.int32)
        is_live = slot_index < tile_count[0]
        chosen = (mode1_column[:, 0][None, :] == jnp.arange(n_col, dtype=jnp.int32)[:, None]) & is_live[None, :]
        chosen = chosen.astype(jnp.float32)
        earlier = (slot_index[:, None] < slot_index[None, :]).astype(jnp.float32)
        rank = jnp.dot(chosen, earlier)
        own_rank = jnp.sum(chosen * rank, axis=0).astype(jnp.int32)
        out_slot = jnp.clip(mode1_column[:, 0], 0, n_col - 1) * SLOTS + own_rank
        table = jnp.stack(
            [
                jnp.clip(mode2_row[:, 0] * JB_DEV + mode2_offset, 0, gathered.shape[0] // tile_edge - 1),
                jnp.clip(mode3_offset, 0, mode3_factor.shape[0] // tile_edge - 1),
                out_slot,
            ]
        ).astype(jnp.int32)
        place = jnp.arange(SLOTS, dtype=jnp.float32)
        taken = chosen[:, None, :] * (rank[:, None, :] == place[None, :, None])
        targets = jnp.sum(taken * (mode1_offset + 1).astype(jnp.float32), axis=2) - 1.0
        target_rows = jnp.zeros((8, rank_width), jnp.float32).at[0, : n_col * SLOTS].set(targets.reshape(-1))

    with jax.named_scope("normal"):
        own_second = gram_of(mode2_factor)
        own_third = gram_of(mode3_factor)
        exchanged = lax.all_to_all(own_second.reshape(n_row, part, rank_width), "row", 0, 0)
        second_part = jnp.sum(exchanged, axis=0)
        third_part = lax.dynamic_slice_in_dim(own_third, row_index * part, part, 0)
        sent = jnp.concatenate([second_part, third_part, target_rows], axis=0)
        spread = lax.all_to_all(jnp.broadcast_to(sent[None], (n_col,) + sent.shape), "col", 0, 0)
        both = jnp.sum(spread[:, : 2 * part], axis=0)
        normal_part = both[:part] * both[part:]
        normal_matrix = lax.all_to_all(
            jnp.broadcast_to(normal_part[None], (n_row, part, rank_width)), "row", 0, 0
        ).reshape(rank_width, rank_width)
        received_targets = lax.dynamic_slice_in_dim(spread[:, 2 * part], col_index * SLOTS, SLOTS, 1)
        received_targets = received_targets.astype(jnp.int32).reshape(-1)

    with jax.named_scope("contract"):
        partials = contract_tiles(
            table,
            tile_count,
            tile_values,
            gathered.reshape(-1, tile_edge, rank_width),
            mode3_factor.reshape(-1, tile_edge, rank_width),
            n_col * SLOTS,
        )
    with jax.named_scope("exchange"):
        received = lax.all_to_all(
            partials.reshape(n_col, SLOTS * tile_edge, rank_width), "col", 0, 0
        ).reshape(n_col * SLOTS, tile_edge, rank_width)

    with jax.named_scope("inverse"):
        inverse = invert(normal_matrix)

    with jax.named_scope("combine"):
        return combine(received_targets, received, inverse)


def solution(mesh):
    placed = (
        P(("row", "col"), None, None),
        P(("row", "col")),
        P(("row", "col"), None),
        P(("row", "col")),
        P(("row", "col"), None),
        P(("row", "col")),
        P(("row", "col")),
        P(("row", "col"), None),
        P("col", None),
    )
    return jax.shard_map(
        local, mesh=mesh, in_specs=placed, out_specs=P(("row", "col"), None), check_vma=False
    )
```

```python
import functools

import jax
import jax.numpy as jnp
from jax import lax
from jax.experimental import pallas as pl
from jax.experimental.pallas import tpu as pltpu
from jax.sharding import PartitionSpec as P

IB_DEV = 16
JB_DEV = 8
SLOTS = 4
PAIR = 2

HIGHEST = lax.Precision.HIGHEST


def gram_of(matrix):
    return lax.dot_general(
        matrix, matrix, (((0,), (0,)), ((), ())), precision=HIGHEST, preferred_element_type=jnp.float32
    )


def split(value):
    high = value.astype(jnp.bfloat16)
    low = (value - high.astype(jnp.float32)).astype(jnp.bfloat16)
    return high, low


def dot32(left, right):
    return jnp.dot(left, right, preferred_element_type=jnp.float32)


def contract_kernel(table_ref, bound_ref, tile_hbm, own_hbm, other_hbm, third_ref, *rest):
    out_hbm, tile_buf, second_buf, result_buf, tile_sem, second_sem, result_sem = rest[-7:]
    low, high = bound_ref[0], bound_ref[1]
    pairs = (high - low + PAIR - 1) // PAIR
    tile_edge = third_ref.shape[1]
    depth = tile_buf.shape[2]
    chunk = min(256, depth)
    per_chunk = chunk // tile_edge

    def tile_copy(at):
        return pltpu.make_async_copy(tile_hbm.at[table_ref[0, at]], tile_buf.at[at], tile_sem.at[at])

    def second_copy(source, at):
        return pltpu.make_async_copy(source.at[table_ref[1, at]], second_buf.at[at], second_sem.at[at])

    def result_copy(at):
        return pltpu.make_async_copy(result_buf.at[at], out_hbm.at[table_ref[3, at]], result_sem.at[at])

    def start(at, carry):
        tile_copy(at).start()
        other = table_ref[4, at]

        @pl.when(other == 0)
        def _():
            second_copy(own_hbm, at).start()

        @pl.when(other != 0)
        def _():
            second_copy(other_hbm, at).start()

        return carry

    lax.fori_loop(low, high, start, 0)

    def contract(pair, carry):
        first = low + pair * PAIR
        for u in range(PAIR):

            @pl.when(first + u < high)
            def _():
                tile_copy(first + u).wait()
                second_copy(own_hbm, first + u).wait()

        for u in range(PAIR):
            at = jnp.minimum(first + u, high - 1)
            second = second_buf[at]
            third = third_ref[table_ref[2, at]]
            high_part, low_part = split(tile_buf[at])
            both = jnp.concatenate([high_part, low_part], axis=0)
            total = jnp.zeros((2 * tile_edge, third.shape[1]), jnp.float32)
            total_low = jnp.zeros((tile_edge, third.shape[1]), jnp.float32)
            for q in range(depth // chunk):
                rows = second[q * per_chunk : (q + 1) * per_chunk]
                khatri = (rows[:, None, :] * third[None, :, :]).reshape(chunk, third.shape[1])
                khatri_high, khatri_low = split(khatri)
                total = total + dot32(both[:, q * chunk : (q + 1) * chunk], khatri_high)
                total_low = total_low + dot32(high_part[:, q * chunk : (q + 1) * chunk], khatri_low)
            result = total[:tile_edge] + (total[tile_edge:] + total_low)

            @pl.when(first + u < high)
            def _():
                result_buf[first + u] = result
                result_copy(first + u).start()

        return carry

    lax.fori_loop(0, pairs, contract, 0)

    def finish(at, carry):
        result_copy(at).wait()
        return carry

    lax.fori_loop(low, high, finish, 0)


def contract_tiles(table, bounds, tile_values, own_blocks, other_blocks, third_blocks, out_slots, earlier=()):
    slot_count, tile_edge, depth = tile_values.shape
    rank_width = third_blocks.shape[2]
    smem = pl.BlockSpec(memory_space=pltpu.SMEM)
    vmem = pl.BlockSpec(memory_space=pltpu.VMEM)
    hbm = pl.BlockSpec(memory_space=pltpu.HBM)
    block = (slot_count, tile_edge, rank_width)
    return pl.pallas_call(
        contract_kernel,
        out_shape=jax.ShapeDtypeStruct((out_slots, tile_edge, rank_width), jnp.float32),
        in_specs=[smem, smem, hbm, hbm, hbm, vmem] + [hbm] * len(earlier),
        out_specs=hbm,
        scratch_shapes=[
            pltpu.VMEM((slot_count, tile_edge, depth), jnp.float32),
            pltpu.VMEM(block, jnp.float32),
            pltpu.VMEM(block, jnp.float32),
            pltpu.SemaphoreType.DMA((slot_count,)),
            pltpu.SemaphoreType.DMA((slot_count,)),
            pltpu.SemaphoreType.DMA((slot_count,)),
        ],
        input_output_aliases={6: 0} if earlier else {},
        compiler_params=pltpu.CompilerParams(vmem_limit_bytes=60 * 1024 * 1024),
        cost_estimate=pl.CostEstimate(
            flops=3 * slot_count * tile_edge * depth * rank_width, bytes_accessed=5_000_000, transcendentals=0
        ),
        name="contract",
    )(table, bounds, tile_values, own_blocks, other_blocks, third_blocks, *earlier)


def combine_kernel(target_ref, received_ref, inverse_ref, out_ref, total_ref):
    tile_edge = received_ref.shape[1]
    total_ref[...] = jnp.zeros_like(total_ref)

    def add(slot, carry):
        target = target_ref[slot]

        @pl.when(target >= 0)
        def _():
            rows = pl.ds(pl.multiple_of(target * tile_edge, tile_edge), tile_edge)
            total_ref[rows, :] += received_ref[slot]

        return carry

    lax.fori_loop(0, received_ref.shape[0], add, 0)
    out_ref[...] = jnp.dot(
        total_ref[...], inverse_ref[...], precision=HIGHEST, preferred_element_type=jnp.float32
    )


def combine(targets, received, inverse):
    tile_edge, rank_width = received.shape[1:]
    vmem = pl.BlockSpec(memory_space=pltpu.VMEM)
    return pl.pallas_call(
        combine_kernel,
        out_shape=jax.ShapeDtypeStruct((IB_DEV * tile_edge, rank_width), jnp.float32),
        in_specs=[pl.BlockSpec(memory_space=pltpu.SMEM), vmem, vmem],
        out_specs=vmem,
        scratch_shapes=[pltpu.VMEM((IB_DEV * tile_edge, rank_width), jnp.float32)],
        compiler_params=pltpu.CompilerParams(vmem_limit_bytes=16 * 1024 * 1024),
        name="combine",
    )(targets, received, inverse)


def invert_four(s):
    det = s[0][0] * s[1][1] - s[0][1] * s[0][1]
    over = 1.0 / det
    a00, a01, a11 = s[1][1] * over, -s[0][1] * over, s[0][0] * over
    y00 = a00 * s[0][2] + a01 * s[1][2]
    y01 = a00 * s[0][3] + a01 * s[1][3]
    y10 = a01 * s[0][2] + a11 * s[1][2]
    y11 = a01 * s[0][3] + a11 * s[1][3]
    c00 = s[2][2] - (s[0][2] * y00 + s[1][2] * y10)
    c01 = s[2][3] - (s[0][2] * y01 + s[1][2] * y11)
    c11 = s[3][3] - (s[0][3] * y01 + s[1][3] * y11)
    over = 1.0 / (c00 * c11 - c01 * c01)
    d00, d01, d11 = c11 * over, -c01 * over, c00 * over
    e00 = -(y00 * d00 + y01 * d01)
    e01 = -(y00 * d01 + y01 * d11)
    e10 = -(y10 * d00 + y11 * d01)
    e11 = -(y10 * d01 + y11 * d11)
    b00 = a00 - (e00 * y00 + e01 * y01)
    b01 = a01 - (e00 * y10 + e01 * y11)
    b11 = a11 - (e10 * y10 + e11 * y11)
    return [[b00, b01, e00, e01], [b01, b11, e10, e11], [e00, e10, d00, d01], [e01, e11, d01, d11]]

def invert_block(groups):
    width = groups[0].shape[1]
    full = (8, width)
    lane = lax.broadcasted_iota(jnp.int32, full, 1)
    sub = lax.broadcasted_iota(jnp.int32, full, 0)
    for first in range(0, width, 4):
        at, off = first // 8, first % 8
        cols = [[jnp.broadcast_to(g[:, first + j : first + j + 1], full) for j in range(4)] for g in groups]
        s = [[jnp.broadcast_to(cols[at][j][off + i : off + i + 1], full) if i <= j else None for j in range(4)] for i in range(4)]
        rows = [jnp.broadcast_to(groups[at][off + i : off + i + 1], full) for i in range(4)]
        d = invert_four(s)
        new_rows = []
        for i in range(4):
            w = d[i][0] * rows[0] + d[i][1] * rows[1] + d[i][2] * rows[2] + d[i][3] * rows[3]
            for j in range(4):
                w = jnp.where(lane == first + j, d[i][j], w)
            new_rows.append(w)
        in_pivot = (lane >= first) & (lane < first + 4)
        out = []
        for k, g in enumerate(groups):
            v = jnp.where(in_pivot, 0.0, g)
            v = v - ((cols[k][0] * new_rows[0] + cols[k][1] * new_rows[1]) + (cols[k][2] * new_rows[2] + cols[k][3] * new_rows[3]))
            if k == at:
                for i in range(4):
                    v = jnp.where(sub == off + i, new_rows[i], v)
            out.append(v)
        groups = out
    return groups

def invert_kernel(block, normal_ref, out_ref, work_ref):
    n = normal_ref.shape[0]
    normal = normal_ref[...]
    on_diagonal = lax.broadcasted_iota(jnp.int32, (n, n), 0) == lax.broadcasted_iota(jnp.int32, (n, n), 1)
    diagonal = jnp.where(on_diagonal, normal, 0.0)
    scale_row = lax.rsqrt(jnp.sum(diagonal, axis=0, keepdims=True))
    scale_col = lax.rsqrt(jnp.sum(diagonal, axis=1, keepdims=True))
    work_ref[...] = normal * scale_col * scale_row
    for first in range(0, n, block):
        last = first + block
        groups = [work_ref[r : r + 8, first:last] for r in range(first, last, 8)]
        inner = jnp.concatenate(invert_block(groups), axis=0)
        rows = jnp.dot(inner, work_ref[first:last, :], precision=HIGHEST, preferred_element_type=jnp.float32)
        pieces = [rows[:, :first]] if first else []
        pieces.append(inner)
        if last < n:
            pieces.append(rows[:, last:])
        rows = jnp.concatenate(pieces, axis=1)
        change = jnp.dot(work_ref[:, first:last], rows, precision=HIGHEST, preferred_element_type=jnp.float32)
        lane = lax.broadcasted_iota(jnp.int32, (n, n), 1)
        work_ref[...] = jnp.where((lane >= first) & (lane < last), 0.0, work_ref[...]) - change
        work_ref[first:last, :] = rows
    out_ref[...] = work_ref[...] * scale_col * scale_row

def invert(normal, block=64):
    n = normal.shape[0]
    vmem = pl.BlockSpec(memory_space=pltpu.VMEM)
    return pl.pallas_call(
        functools.partial(invert_kernel, block),
        out_shape=jax.ShapeDtypeStruct((n, n), jnp.float32),
        in_specs=[vmem], out_specs=vmem,
        scratch_shapes=[pltpu.VMEM((n, n), jnp.float32)],
        compiler_params=pltpu.CompilerParams(vmem_limit_bytes=16 * 1024 * 1024),
        cost_estimate=pl.CostEstimate(flops=12 * n * n * n, bytes_accessed=8 * n * n, transcendentals=0),
        name="invert",
    )(normal)


def local(
    tile_values,
    tile_count,
    mode1_column,
    mode1_offset,
    mode2_row,
    mode2_offset,
    mode3_offset,
    mode2_factor,
    mode3_factor,
):
    slot_count, tile_edge, _ = tile_values.shape
    rank_width = mode2_factor.shape[1]
    row_index = lax.axis_index("row")
    col_index = lax.axis_index("col")
    n_row = lax.axis_size("row")
    n_col = lax.axis_size("col")
    part = rank_width // n_row

    with jax.named_scope("normal"):
        own_second = gram_of(mode2_factor)
        exchanged = lax.all_to_all(own_second.reshape(n_row, part, rank_width), "row", 0, 0)

    with jax.named_scope("gather_second"):
        n_z = n_row // 2

        def moved(shift):
            pairs = [(i, 2 * ((i // 2 + shift) % n_z) + i % 2) for i in range(n_row)]
            return lax.ppermute(mode2_factor, "row", pairs)

        near = [1, n_z - 1, 2, n_z - 2]
        far = [3, n_z - 3, 4]
        twin = [(i, i ^ 1) for i in range(n_row)]
        near_own = jnp.concatenate([mode2_factor] + [moved(shift) for shift in near], axis=0)
        far_own = jnp.concatenate([moved(shift) for shift in far], axis=0)
        near_other = lax.ppermute(near_own, "row", twin)
        far_other = lax.ppermute(far_own, "row", twin)

    with jax.named_scope("tables"):
        slot_index = jnp.arange(slot_count, dtype=jnp.int32)
        live_count = tile_count[0]
        is_live = slot_index < live_count
        chosen = (mode1_column[:, 0][None, :] == jnp.arange(n_col, dtype=jnp.int32)[:, None]) & is_live[None, :]
        chosen = chosen.astype(jnp.float32)
        earlier = (slot_index[:, None] < slot_index[None, :]).astype(jnp.float32)
        rank = jnp.dot(chosen, earlier)
        own_rank = jnp.sum(chosen * rank, axis=0).astype(jnp.int32)
        out_slot = jnp.clip(mode1_column[:, 0], 0, n_col - 1) * SLOTS + own_rank
        source = jnp.clip(mode2_row[:, 0], 0, n_row - 1)
        shift = (row_index // 2 - source // 2 + n_z) % n_z
        place_of = [0] * n_z
        for at, each in enumerate([0] + near):
            place_of[each] = at
        for at, each in enumerate(far):
            place_of[each] = at
        place = sum(jnp.where(shift == each, place_of[each], 0) for each in range(n_z))
        is_far = (shift > 2) & (shift < n_z - 2)
        is_other = (source % 2 != row_index % 2).astype(jnp.int32)
        group = jnp.where(is_live, is_far.astype(jnp.int32), 2)
        before = (group[:, None] < group[None, :]) | (
            (group[:, None] == group[None, :]) & (slot_index[:, None] < slot_index[None, :])
        )
        position = jnp.sum(before.astype(jnp.int32), axis=0)
        table = jnp.stack(
            [
                slot_index,
                place * JB_DEV + jnp.clip(mode2_offset, 0, JB_DEV - 1),
                jnp.clip(mode3_offset, 0, mode3_factor.shape[0] // tile_edge - 1),
                out_slot,
                is_other,
            ]
        )
        table = jnp.sum(
            jnp.where(position[None, :, None] == slot_index[None, None, :], table[:, :, None], 0), axis=1
        ).astype(jnp.int32)
        near_count = jnp.sum((group == 0).astype(jnp.int32))
        near_bounds = jnp.stack([jnp.int32(0), near_count]).astype(jnp.int32)
        far_bounds = jnp.stack([near_count, live_count]).astype(jnp.int32)
        slots = jnp.arange(SLOTS, dtype=jnp.float32)
        taken = chosen[:, None, :] * (rank[:, None, :] == slots[None, :, None])
        targets = jnp.sum(taken * (mode1_offset + 1).astype(jnp.float32), axis=2) - 1.0
        target_rows = jnp.zeros((8, rank_width), jnp.float32).at[0, : n_col * SLOTS].set(targets.reshape(-1))

    with jax.named_scope("normal"):
        own_third = gram_of(mode3_factor)
        second_part = jnp.sum(exchanged, axis=0)
        third_part = lax.dynamic_slice_in_dim(own_third, row_index * part, part, 0)
        sent = jnp.concatenate([second_part, third_part, target_rows], axis=0)
        spread = lax.all_to_all(jnp.broadcast_to(sent[None], (n_col,) + sent.shape), "col", 0, 0)
        both = jnp.sum(spread[:, : 2 * part], axis=0)
        normal_part = both[:part] * both[part:]
        normal_matrix = lax.all_to_all(
            jnp.broadcast_to(normal_part[None], (n_row, part, rank_width)), "row", 0, 0
        ).reshape(rank_width, rank_width)
        received_targets = lax.dynamic_slice_in_dim(spread[:, 2 * part], col_index * SLOTS, SLOTS, 1)
        received_targets = received_targets.astype(jnp.int32).reshape(-1)

    with jax.named_scope("contract"):
        third_blocks = mode3_factor.reshape(-1, tile_edge, rank_width)

        def blocks(array):
            return array.reshape(-1, tile_edge, rank_width)

        out_slots = n_col * SLOTS
        near_done = contract_tiles(
            table, near_bounds, tile_values, blocks(near_own), blocks(near_other), third_blocks, out_slots
        )
        partials = contract_tiles(
            table, far_bounds, tile_values, blocks(far_own), blocks(far_other), third_blocks, out_slots, (near_done,)
        )
    with jax.named_scope("exchange"):
        received = lax.all_to_all(
            partials.reshape(n_col, SLOTS * tile_edge, rank_width), "col", 0, 0
        ).reshape(n_col * SLOTS, tile_edge, rank_width)

    with jax.named_scope("inverse"):
        inverse = invert(normal_matrix)

    with jax.named_scope("combine"):
        return combine(received_targets, received, inverse)


def solution(mesh):
    placed = (
        P(("row", "col"), None, None),
        P(("row", "col")),
        P(("row", "col"), None),
        P(("row", "col")),
        P(("row", "col"), None),
        P(("row", "col")),
        P(("row", "col")),
        P(("row", "col"), None),
        P("col", None),
    )
    return jax.shard_map(
        local, mesh=mesh, in_specs=placed, out_specs=P(("row", "col"), None), check_vma=False
    )
```

```python
import functools

import jax
import jax.numpy as jnp
from jax import lax
from jax.experimental import pallas as pl
from jax.experimental.pallas import tpu as pltpu
from jax.sharding import PartitionSpec as P

IB_DEV = 16
JB_DEV = 8
SLOTS = 4
PAIR = 2

HIGHEST = lax.Precision.HIGHEST


def gram_of(matrix):
    return lax.dot_general(
        matrix, matrix, (((0,), (0,)), ((), ())), precision=HIGHEST, preferred_element_type=jnp.float32
    )


def split(value):
    high = value.astype(jnp.bfloat16)
    low = (value - high.astype(jnp.float32)).astype(jnp.bfloat16)
    return high, low


def dot32(left, right):
    return jnp.dot(left, right, preferred_element_type=jnp.float32)


def contract_kernel(
    table_ref,
    count_ref,
    tile_hbm,
    third_ref,
    source_0,
    source_1,
    source_2,
    source_3,
    out_hbm,
    tile_buf,
    second_buf,
    result_buf,
    tile_sem,
    second_sem,
    result_sem,
):
    count = count_ref[0]
    pairs = (count + PAIR - 1) // PAIR
    tile_edge = third_ref.shape[1]
    depth = tile_buf.shape[2]
    chunk = min(256, depth)
    per_chunk = chunk // tile_edge

    def tile_copy(pair):
        return pltpu.make_async_copy(
            tile_hbm.at[pl.ds(pair * PAIR, PAIR)], tile_buf.at[pl.ds(pair * PAIR, PAIR)], tile_sem.at[pair]
        )

    sources = [source_0, source_1, source_2, source_3]

    def second_copy(source, slot):
        return pltpu.make_async_copy(source.at[table_ref[0, slot]], second_buf.at[slot], second_sem.at[slot])

    def result_copy(slot):
        return pltpu.make_async_copy(result_buf.at[slot], out_hbm.at[table_ref[2, slot]], result_sem.at[slot])

    def start(pair, carry):
        tile_copy(pair).start()
        for at in range(PAIR):
            slot = pair * PAIR + at
            chosen = table_ref[3, slot]
            for which, source in enumerate(sources):

                @pl.when(chosen == which)
                def _():
                    second_copy(source, slot).start()

        return carry

    lax.fori_loop(0, pairs, start, 0)

    def contract(pair, carry):
        tile_copy(pair).wait()
        for at in range(PAIR):
            second_copy(source_0, pair * PAIR + at).wait()
        for at in range(PAIR):
            slot = pair * PAIR + at
            second = second_buf[slot]
            third = third_ref[table_ref[1, slot]]
            high, low = split(tile_buf[slot])
            both = jnp.concatenate([high, low], axis=0)
            total = jnp.zeros((2 * tile_edge, third.shape[1]), jnp.float32)
            total_low = jnp.zeros((tile_edge, third.shape[1]), jnp.float32)
            for q in range(depth // chunk):
                rows = second[q * per_chunk : (q + 1) * per_chunk]
                khatri = (rows[:, None, :] * third[None, :, :]).reshape(chunk, third.shape[1])
                khatri_high, khatri_low = split(khatri)
                total = total + dot32(both[:, q * chunk : (q + 1) * chunk], khatri_high)
                total_low = total_low + dot32(high[:, q * chunk : (q + 1) * chunk], khatri_low)
            result_buf[slot] = total[:tile_edge] + (total[tile_edge:] + total_low)

            @pl.when(slot < count)
            def _():
                result_copy(slot).start()

        return carry

    lax.fori_loop(0, pairs, contract, 0)

    def finish(slot, carry):
        result_copy(slot).wait()
        return carry

    lax.fori_loop(0, count, finish, 0)


def contract_tiles(table, count, tile_values, third_blocks, sources, out_slots):
    slot_count, tile_edge, depth = tile_values.shape
    rank_width = third_blocks.shape[2]
    smem = pl.BlockSpec(memory_space=pltpu.SMEM)
    vmem = pl.BlockSpec(memory_space=pltpu.VMEM)
    hbm = pl.BlockSpec(memory_space=pltpu.HBM)
    return pl.pallas_call(
        contract_kernel,
        out_shape=jax.ShapeDtypeStruct((out_slots, tile_edge, rank_width), jnp.float32),
        in_specs=[smem, smem, hbm, vmem] + [hbm] * len(sources),
        out_specs=hbm,
        scratch_shapes=[
            pltpu.VMEM((slot_count, tile_edge, depth), jnp.float32),
            pltpu.VMEM((slot_count, tile_edge, rank_width), jnp.float32),
            pltpu.VMEM((slot_count, tile_edge, rank_width), jnp.float32),
            pltpu.SemaphoreType.DMA((slot_count // PAIR,)),
            pltpu.SemaphoreType.DMA((slot_count,)),
            pltpu.SemaphoreType.DMA((slot_count,)),
        ],
        compiler_params=pltpu.CompilerParams(vmem_limit_bytes=60 * 1024 * 1024),
        cost_estimate=pl.CostEstimate(
            flops=6 * slot_count * tile_edge * depth * rank_width, bytes_accessed=10_000_000, transcendentals=0
        ),
        name="contract",
    )(table, count, tile_values, third_blocks, *sources)


def combine_kernel(target_ref, received_ref, inverse_ref, out_ref, total_ref):
    tile_edge = received_ref.shape[1]
    total_ref[...] = jnp.zeros_like(total_ref)

    def add(slot, carry):
        target = target_ref[slot]

        @pl.when(target >= 0)
        def _():
            rows = pl.ds(pl.multiple_of(target * tile_edge, tile_edge), tile_edge)
            total_ref[rows, :] += received_ref[slot]

        return carry

    lax.fori_loop(0, received_ref.shape[0], add, 0)
    out_ref[...] = jnp.dot(
        total_ref[...], inverse_ref[...], precision=HIGHEST, preferred_element_type=jnp.float32
    )


def combine(targets, received, inverse):
    tile_edge, rank_width = received.shape[1:]
    vmem = pl.BlockSpec(memory_space=pltpu.VMEM)
    return pl.pallas_call(
        combine_kernel,
        out_shape=jax.ShapeDtypeStruct((IB_DEV * tile_edge, rank_width), jnp.float32),
        in_specs=[pl.BlockSpec(memory_space=pltpu.SMEM), vmem, vmem],
        out_specs=vmem,
        scratch_shapes=[pltpu.VMEM((IB_DEV * tile_edge, rank_width), jnp.float32)],
        compiler_params=pltpu.CompilerParams(vmem_limit_bytes=16 * 1024 * 1024),
        name="combine",
    )(targets, received, inverse)


def invert_four(s):
    det = s[0][0] * s[1][1] - s[0][1] * s[0][1]
    over = 1.0 / det
    a00, a01, a11 = s[1][1] * over, -s[0][1] * over, s[0][0] * over
    y00 = a00 * s[0][2] + a01 * s[1][2]
    y01 = a00 * s[0][3] + a01 * s[1][3]
    y10 = a01 * s[0][2] + a11 * s[1][2]
    y11 = a01 * s[0][3] + a11 * s[1][3]
    c00 = s[2][2] - (s[0][2] * y00 + s[1][2] * y10)
    c01 = s[2][3] - (s[0][2] * y01 + s[1][2] * y11)
    c11 = s[3][3] - (s[0][3] * y01 + s[1][3] * y11)
    over = 1.0 / (c00 * c11 - c01 * c01)
    d00, d01, d11 = c11 * over, -c01 * over, c00 * over
    e00 = -(y00 * d00 + y01 * d01)
    e01 = -(y00 * d01 + y01 * d11)
    e10 = -(y10 * d00 + y11 * d01)
    e11 = -(y10 * d01 + y11 * d11)
    b00 = a00 - (e00 * y00 + e01 * y01)
    b01 = a01 - (e00 * y10 + e01 * y11)
    b11 = a11 - (e10 * y10 + e11 * y11)
    return [[b00, b01, e00, e01], [b01, b11, e10, e11], [e00, e10, d00, d01], [e01, e11, d01, d11]]

def invert_block(groups):
    width = groups[0].shape[1]
    full = (8, width)
    lane = lax.broadcasted_iota(jnp.int32, full, 1)
    sub = lax.broadcasted_iota(jnp.int32, full, 0)
    for first in range(0, width, 4):
        at, off = first // 8, first % 8
        cols = [[jnp.broadcast_to(g[:, first + j : first + j + 1], full) for j in range(4)] for g in groups]
        s = [[jnp.broadcast_to(cols[at][j][off + i : off + i + 1], full) if i <= j else None for j in range(4)] for i in range(4)]
        rows = [jnp.broadcast_to(groups[at][off + i : off + i + 1], full) for i in range(4)]
        d = invert_four(s)
        new_rows = []
        for i in range(4):
            w = d[i][0] * rows[0] + d[i][1] * rows[1] + d[i][2] * rows[2] + d[i][3] * rows[3]
            for j in range(4):
                w = jnp.where(lane == first + j, d[i][j], w)
            new_rows.append(w)
        in_pivot = (lane >= first) & (lane < first + 4)
        out = []
        for k, g in enumerate(groups):
            v = jnp.where(in_pivot, 0.0, g)
            v = v - ((cols[k][0] * new_rows[0] + cols[k][1] * new_rows[1]) + (cols[k][2] * new_rows[2] + cols[k][3] * new_rows[3]))
            if k == at:
                for i in range(4):
                    v = jnp.where(sub == off + i, new_rows[i], v)
            out.append(v)
        groups = out
    return groups

def invert_kernel(block, normal_ref, out_ref, work_ref):
    n = normal_ref.shape[0]
    normal = normal_ref[...]
    on_diagonal = lax.broadcasted_iota(jnp.int32, (n, n), 0) == lax.broadcasted_iota(jnp.int32, (n, n), 1)
    diagonal = jnp.where(on_diagonal, normal, 0.0)
    scale_row = lax.rsqrt(jnp.sum(diagonal, axis=0, keepdims=True))
    scale_col = lax.rsqrt(jnp.sum(diagonal, axis=1, keepdims=True))
    work_ref[...] = normal * scale_col * scale_row
    for first in range(0, n, block):
        last = first + block
        groups = [work_ref[r : r + 8, first:last] for r in range(first, last, 8)]
        inner = jnp.concatenate(invert_block(groups), axis=0)
        rows = jnp.dot(inner, work_ref[first:last, :], precision=HIGHEST, preferred_element_type=jnp.float32)
        pieces = [rows[:, :first]] if first else []
        pieces.append(inner)
        if last < n:
            pieces.append(rows[:, last:])
        rows = jnp.concatenate(pieces, axis=1)
        change = jnp.dot(work_ref[:, first:last], rows, precision=HIGHEST, preferred_element_type=jnp.float32)
        lane = lax.broadcasted_iota(jnp.int32, (n, n), 1)
        work_ref[...] = jnp.where((lane >= first) & (lane < last), 0.0, work_ref[...]) - change
        work_ref[first:last, :] = rows
    out_ref[...] = work_ref[...] * scale_col * scale_row

def invert(normal, block=64):
    n = normal.shape[0]
    vmem = pl.BlockSpec(memory_space=pltpu.VMEM)
    return pl.pallas_call(
        functools.partial(invert_kernel, block),
        out_shape=jax.ShapeDtypeStruct((n, n), jnp.float32),
        in_specs=[vmem], out_specs=vmem,
        scratch_shapes=[pltpu.VMEM((n, n), jnp.float32)],
        compiler_params=pltpu.CompilerParams(vmem_limit_bytes=16 * 1024 * 1024),
        cost_estimate=pl.CostEstimate(flops=12 * n * n * n, bytes_accessed=8 * n * n, transcendentals=0),
        name="invert",
    )(normal)


def local(
    tile_values,
    tile_count,
    mode1_column,
    mode1_offset,
    mode2_row,
    mode2_offset,
    mode3_offset,
    mode2_factor,
    mode3_factor,
):
    slot_count, tile_edge, _ = tile_values.shape
    rank_width = mode2_factor.shape[1]
    row_index = lax.axis_index("row")
    col_index = lax.axis_index("col")
    n_row = lax.axis_size("row")
    n_col = lax.axis_size("col")
    part = rank_width // n_col

    with jax.named_scope("gather_second"):
        n_z = n_row // 2

        def moved(shift):
            pairs = [(i, 2 * ((i // 2 + shift) % n_z) + i % 2) for i in range(n_row)]
            return lax.ppermute(mode2_factor, "row", pairs)

        near = [1, n_z - 1, 2, n_z - 2]
        far = [3, n_z - 3, 4]
        twin = [(i, i ^ 1) for i in range(n_row)]
        near_own = jnp.concatenate([mode2_factor] + [moved(shift) for shift in near], axis=0)
        far_own = jnp.concatenate([moved(shift) for shift in far], axis=0)
        near_other = lax.ppermute(near_own, "row", twin)
        far_other = lax.ppermute(far_own, "row", twin)

    with jax.named_scope("tables"):
        slot_index = jnp.arange(slot_count, dtype=jnp.int32)
        is_live = slot_index < tile_count[0]
        chosen = (mode1_column[:, 0][None, :] == jnp.arange(n_col, dtype=jnp.int32)[:, None]) & is_live[None, :]
        chosen = chosen.astype(jnp.float32)
        earlier = (slot_index[:, None] < slot_index[None, :]).astype(jnp.float32)
        rank = jnp.dot(chosen, earlier)
        own_rank = jnp.sum(chosen * rank, axis=0).astype(jnp.int32)
        out_slot = jnp.clip(mode1_column[:, 0], 0, n_col - 1) * SLOTS + own_rank
        source = jnp.clip(mode2_row[:, 0], 0, n_row - 1)
        shift = (row_index // 2 - source // 2 + n_z) % n_z
        place_of = [0] * n_z
        for at, each in enumerate([0] + near):
            place_of[each] = at
        for at, each in enumerate(far):
            place_of[each] = at
        place = sum(jnp.where(shift == each, place_of[each], 0) for each in range(n_z))
        is_far = ((shift > 2) & (shift < n_z - 2)).astype(jnp.int32)
        is_other = (source % 2 != row_index % 2).astype(jnp.int32)
        table = jnp.stack(
            [
                place * JB_DEV + jnp.clip(mode2_offset, 0, JB_DEV - 1),
                jnp.clip(mode3_offset, 0, mode3_factor.shape[0] // tile_edge - 1),
                out_slot,
                is_far + 2 * is_other,
            ]
        ).astype(jnp.int32)
        slots = jnp.arange(SLOTS, dtype=jnp.float32)
        taken = chosen[:, None, :] * (rank[:, None, :] == slots[None, :, None])
        targets = jnp.sum(taken * (mode1_offset + 1).astype(jnp.float32), axis=2) - 1.0
        target_rows = jnp.zeros((8, rank_width), jnp.float32).at[0, : n_col * SLOTS].set(targets.reshape(-1))

    with jax.named_scope("normal"):
        strips = [gram_of(each).reshape(n_col, part, rank_width) for each in (mode2_factor, mode3_factor)]
        strips = lax.all_to_all(jnp.concatenate(strips, axis=1), "col", 0, 0)
        strips = jnp.sum(strips, axis=0)
        second_strips = lax.all_to_all(
            jnp.broadcast_to(strips[None, :part], (n_row, part, rank_width)), "row", 0, 0
        )
        normal_part = jnp.sum(second_strips, axis=0) * strips[part:]
        sent = jnp.concatenate([normal_part, target_rows], axis=0)
        spread = lax.all_to_all(jnp.broadcast_to(sent[None], (n_col,) + sent.shape), "col", 0, 0)
        normal_matrix = spread[:, :part].reshape(rank_width, rank_width)
        received_targets = lax.dynamic_slice_in_dim(spread[:, part], col_index * SLOTS, SLOTS, 1)
        received_targets = received_targets.astype(jnp.int32).reshape(-1)

    with jax.named_scope("contract"):
        def blocks(array):
            return array.reshape(-1, tile_edge, rank_width)

        partials = contract_tiles(
            table,
            tile_count,
            tile_values,
            blocks(mode3_factor),
            [blocks(near_own), blocks(far_own), blocks(near_other), blocks(far_other)],
            n_col * SLOTS,
        )
    with jax.named_scope("exchange"):
        received = lax.all_to_all(
            partials.reshape(n_col, SLOTS * tile_edge, rank_width), "col", 0, 0
        ).reshape(n_col * SLOTS, tile_edge, rank_width)

    with jax.named_scope("inverse"):
        inverse = invert(normal_matrix)

    with jax.named_scope("combine"):
        return combine(received_targets, received, inverse)


def solution(mesh):
    placed = (
        P(("row", "col"), None, None),
        P(("row", "col")),
        P(("row", "col"), None),
        P(("row", "col")),
        P(("row", "col"), None),
        P(("row", "col")),
        P(("row", "col")),
        P(("row", "col"), None),
        P("col", None),
    )
    return jax.shard_map(
        local, mesh=mesh, in_specs=placed, out_specs=P(("row", "col"), None), check_vma=False
    )
```

```python
import functools

import jax
import jax.numpy as jnp
from jax import lax
from jax.experimental import pallas as pl
from jax.experimental.pallas import tpu as pltpu
from jax.sharding import PartitionSpec as P

IB_DEV = 16
JB_DEV = 8
SLOTS = 4
GROUP = 4
AHEAD = 2

HIGHEST = lax.Precision.HIGHEST


def gram_of(matrix):
    return lax.dot_general(
        matrix, matrix, (((0,), (0,)), ((), ())), precision=HIGHEST, preferred_element_type=jnp.float32
    )


def split(value):
    high = value.astype(jnp.bfloat16)
    low = (value - high.astype(jnp.float32)).astype(jnp.bfloat16)
    return high, low


def dot32(left, right):
    return jnp.dot(left, right, preferred_element_type=jnp.float32)


def contract_kernel(table_ref, count_ref, tile_hbm, third_ref, *rest):
    sources, rest = rest[:-7], rest[-7:]
    out_hbm, tile_buf, second_buf, result_buf, tile_sem, second_sem, result_sem = rest
    count = count_ref[0]
    groups = (count + GROUP - 1) // GROUP
    slot_count, tile_edge, depth = tile_hbm.shape
    chunk = min(256, depth)
    per_chunk = chunk // tile_edge

    def tile_copy(group):
        span = pl.ds(group * GROUP, GROUP)
        return pltpu.make_async_copy(tile_hbm.at[span], tile_buf.at[span], tile_sem.at[group])

    def second_copy(source, slot):
        return pltpu.make_async_copy(source.at[table_ref[0, slot]], second_buf.at[slot], second_sem.at[slot])

    def result_copy(slot):
        return pltpu.make_async_copy(result_buf.at[slot], out_hbm.at[table_ref[2, slot]], result_sem.at[slot])

    def start(group):
        tile_copy(group).start()
        for at in range(GROUP):
            slot = group * GROUP + at
            if len(sources) == 1:
                second_copy(sources[0], slot).start()
            else:
                chosen = table_ref[3, slot]
                for which, source in enumerate(sources):

                    @pl.when(chosen == which)
                    def _():
                        second_copy(source, slot).start()

    for group in range(AHEAD):

        @pl.when(group < groups)
        def _():
            start(group)

    def contract(group, carry):
        @pl.when(group + AHEAD < groups)
        def _():
            start(group + AHEAD)

        tile_copy(group).wait()
        for at in range(GROUP):
            second_copy(sources[0], group * GROUP + at).wait()
        for at in range(GROUP):
            slot = group * GROUP + at
            second = second_buf[slot]
            third = third_ref[table_ref[1, slot]]
            high, low = split(tile_buf[slot])
            both = jnp.concatenate([high, low], axis=0)
            total = jnp.zeros((2 * tile_edge, third.shape[1]), jnp.float32)
            total_low = jnp.zeros((tile_edge, third.shape[1]), jnp.float32)
            for q in range(depth // chunk):
                rows = second[q * per_chunk : (q + 1) * per_chunk]
                khatri = (rows[:, None, :] * third[None, :, :]).reshape(chunk, third.shape[1])
                khatri_high, khatri_low = split(khatri)
                total = total + dot32(both[:, q * chunk : (q + 1) * chunk], khatri_high)
                total_low = total_low + dot32(high[:, q * chunk : (q + 1) * chunk], khatri_low)
            result_buf[slot] = total[:tile_edge] + (total[tile_edge:] + total_low)
        for at in range(GROUP):
            slot = group * GROUP + at

            @pl.when(slot < count)
            def _():
                result_copy(slot).start()

        return carry

    lax.fori_loop(0, groups, contract, 0)

    def finish(slot, carry):
        result_copy(slot).wait()
        return carry

    lax.fori_loop(0, count, finish, 0)


def contract_tiles(table, count, tile_values, third_blocks, sources, out_slots):
    slot_count, tile_edge, depth = tile_values.shape
    rank_width = third_blocks.shape[2]
    smem = pl.BlockSpec(memory_space=pltpu.SMEM)
    vmem = pl.BlockSpec(memory_space=pltpu.VMEM)
    hbm = pl.BlockSpec(memory_space=pltpu.HBM)
    block = (slot_count, tile_edge, rank_width)
    return pl.pallas_call(
        contract_kernel,
        out_shape=jax.ShapeDtypeStruct((out_slots, tile_edge, rank_width), jnp.float32),
        in_specs=[smem, smem, hbm, vmem] + [hbm] * len(sources),
        out_specs=hbm,
        scratch_shapes=[
            pltpu.VMEM((slot_count, tile_edge, depth), jnp.float32),
            pltpu.VMEM(block, jnp.float32),
            pltpu.VMEM(block, jnp.float32),
            pltpu.SemaphoreType.DMA((slot_count // GROUP,)),
            pltpu.SemaphoreType.DMA((slot_count,)),
            pltpu.SemaphoreType.DMA((slot_count,)),
        ],
        compiler_params=pltpu.CompilerParams(vmem_limit_bytes=60 * 1024 * 1024),
        cost_estimate=pl.CostEstimate(
            flops=6 * slot_count * tile_edge * depth * rank_width, bytes_accessed=10_000_000, transcendentals=0
        ),
        name="contract",
    )(table, count, tile_values, third_blocks, *sources)


def combine_kernel(target_ref, received_ref, inverse_ref, out_ref, total_ref):
    slot_count, tile_edge, _ = received_ref.shape
    total_ref[...] = jnp.zeros_like(total_ref)

    def add(step, carry):
        for at in range(8):
            slot = step * 8 + at
            target = target_ref[slot]
            rows = pl.ds(pl.multiple_of(jnp.maximum(target, 0) * tile_edge, tile_edge), tile_edge)

            @pl.when(target >= 0)
            def _():
                total_ref[rows, :] += received_ref[slot]

        return carry

    lax.fori_loop(0, slot_count // 8, add, 0)
    high, low = split(total_ref[...])
    inverse_high, inverse_low = split(inverse_ref[...])
    out_ref[...] = dot32(high, inverse_high) + (dot32(low, inverse_high) + dot32(high, inverse_low))


def combine(targets, received, inverse):
    tile_edge, rank_width = received.shape[1:]
    vmem = pl.BlockSpec(memory_space=pltpu.VMEM)
    return pl.pallas_call(
        combine_kernel,
        out_shape=jax.ShapeDtypeStruct((IB_DEV * tile_edge, rank_width), jnp.float32),
        in_specs=[pl.BlockSpec(memory_space=pltpu.SMEM), vmem, vmem],
        out_specs=vmem,
        scratch_shapes=[pltpu.VMEM((IB_DEV * tile_edge, rank_width), jnp.float32)],
        compiler_params=pltpu.CompilerParams(vmem_limit_bytes=16 * 1024 * 1024),
        name="combine",
    )(targets, received, inverse)


def invert_four(s):
    det = s[0][0] * s[1][1] - s[0][1] * s[0][1]
    over = 1.0 / det
    a00, a01, a11 = s[1][1] * over, -s[0][1] * over, s[0][0] * over
    y00 = a00 * s[0][2] + a01 * s[1][2]
    y01 = a00 * s[0][3] + a01 * s[1][3]
    y10 = a01 * s[0][2] + a11 * s[1][2]
    y11 = a01 * s[0][3] + a11 * s[1][3]
    c00 = s[2][2] - (s[0][2] * y00 + s[1][2] * y10)
    c01 = s[2][3] - (s[0][2] * y01 + s[1][2] * y11)
    c11 = s[3][3] - (s[0][3] * y01 + s[1][3] * y11)
    over = 1.0 / (c00 * c11 - c01 * c01)
    d00, d01, d11 = c11 * over, -c01 * over, c00 * over
    e00 = -(y00 * d00 + y01 * d01)
    e01 = -(y00 * d01 + y01 * d11)
    e10 = -(y10 * d00 + y11 * d01)
    e11 = -(y10 * d01 + y11 * d11)
    b00 = a00 - (e00 * y00 + e01 * y01)
    b01 = a01 - (e00 * y10 + e01 * y11)
    b11 = a11 - (e10 * y10 + e11 * y11)
    return [[b00, b01, e00, e01], [b01, b11, e10, e11], [e00, e10, d00, d01], [e01, e11, d01, d11]]

def invert_block(groups):
    width = groups[0].shape[1]
    full = (8, width)
    lane = lax.broadcasted_iota(jnp.int32, full, 1)
    sub = lax.broadcasted_iota(jnp.int32, full, 0)
    for first in range(0, width, 4):
        at, off = first // 8, first % 8
        cols = [[jnp.broadcast_to(g[:, first + j : first + j + 1], full) for j in range(4)] for g in groups]
        s = [[jnp.broadcast_to(cols[at][j][off + i : off + i + 1], full) if i <= j else None for j in range(4)] for i in range(4)]
        rows = [jnp.broadcast_to(groups[at][off + i : off + i + 1], full) for i in range(4)]
        d = invert_four(s)
        new_rows = []
        for i in range(4):
            w = d[i][0] * rows[0] + d[i][1] * rows[1] + d[i][2] * rows[2] + d[i][3] * rows[3]
            for j in range(4):
                w = jnp.where(lane == first + j, d[i][j], w)
            new_rows.append(w)
        in_pivot = (lane >= first) & (lane < first + 4)
        out = []
        for k, g in enumerate(groups):
            v = jnp.where(in_pivot, 0.0, g)
            v = v - ((cols[k][0] * new_rows[0] + cols[k][1] * new_rows[1]) + (cols[k][2] * new_rows[2] + cols[k][3] * new_rows[3]))
            if k == at:
                for i in range(4):
                    v = jnp.where(sub == off + i, new_rows[i], v)
            out.append(v)
        groups = out
    return groups

def invert_kernel(block, normal_ref, out_ref, work_ref):
    n = normal_ref.shape[0]
    normal = normal_ref[...]
    on_diagonal = lax.broadcasted_iota(jnp.int32, (n, n), 0) == lax.broadcasted_iota(jnp.int32, (n, n), 1)
    diagonal = jnp.where(on_diagonal, normal, 0.0)
    scale_row = lax.rsqrt(jnp.sum(diagonal, axis=0, keepdims=True))
    scale_col = lax.rsqrt(jnp.sum(diagonal, axis=1, keepdims=True))
    work_ref[...] = normal * scale_col * scale_row
    for first in range(0, n, block):
        last = first + block
        groups = [work_ref[r : r + 8, first:last] for r in range(first, last, 8)]
        inner = jnp.concatenate(invert_block(groups), axis=0)
        rows = jnp.dot(inner, work_ref[first:last, :], precision=HIGHEST, preferred_element_type=jnp.float32)
        pieces = [rows[:, :first]] if first else []
        pieces.append(inner)
        if last < n:
            pieces.append(rows[:, last:])
        rows = jnp.concatenate(pieces, axis=1)
        change = jnp.dot(work_ref[:, first:last], rows, precision=HIGHEST, preferred_element_type=jnp.float32)
        lane = lax.broadcasted_iota(jnp.int32, (n, n), 1)
        work_ref[...] = jnp.where((lane >= first) & (lane < last), 0.0, work_ref[...]) - change
        work_ref[first:last, :] = rows
    out_ref[...] = work_ref[...] * scale_col * scale_row

def invert(normal, block=64):
    n = normal.shape[0]
    vmem = pl.BlockSpec(memory_space=pltpu.VMEM)
    return pl.pallas_call(
        functools.partial(invert_kernel, block),
        out_shape=jax.ShapeDtypeStruct((n, n), jnp.float32),
        in_specs=[vmem], out_specs=vmem,
        scratch_shapes=[pltpu.VMEM((n, n), jnp.float32)],
        compiler_params=pltpu.CompilerParams(vmem_limit_bytes=16 * 1024 * 1024),
        cost_estimate=pl.CostEstimate(flops=12 * n * n * n, bytes_accessed=8 * n * n, transcendentals=0),
        name="invert",
    )(normal)


def local(
    tile_values,
    tile_count,
    mode1_column,
    mode1_offset,
    mode2_row,
    mode2_offset,
    mode3_offset,
    mode2_factor,
    mode3_factor,
):
    slot_count, tile_edge, _ = tile_values.shape
    rank_width = mode2_factor.shape[1]
    row_index = lax.axis_index("row")
    col_index = lax.axis_index("col")
    n_row = lax.axis_size("row")
    n_col = lax.axis_size("col")
    part = rank_width // n_col

    with jax.named_scope("gather_second"):
        n_z = n_row // 2

        def moved(array, shift):
            pairs = [(i, 2 * ((i // 2 + shift) % n_z) + i % 2) for i in range(n_row)]
            return lax.ppermute(array, "row", pairs)

        near = [1, n_z - 1, 2, n_z - 2]
        far = [3, n_z - 3, 4]
        twin = [(i, i ^ 1) for i in range(n_row)]
        up_1, down_1 = moved(mode2_factor, 1), moved(mode2_factor, -1)
        up_2, down_2 = moved(up_1, 1), moved(down_1, -1)
        up_3, down_3 = moved(up_2, 1), moved(down_2, -1)
        middle = mode2_factor.shape[0] // 2
        up_4, down_4 = moved(up_3[:middle], 1), moved(down_3[middle:], -1)
        near_own = jnp.concatenate([mode2_factor, up_1, down_1, up_2, down_2], axis=0)
        far_own = jnp.concatenate([up_3, down_3, up_4, down_4], axis=0)
        near_other = lax.ppermute(near_own, "row", twin)
        far_other = lax.ppermute(far_own, "row", twin)

    with jax.named_scope("tables"):
        slot_index = jnp.arange(slot_count, dtype=jnp.int32)
        is_live = slot_index < tile_count[0]
        chosen = (mode1_column[:, 0][None, :] == jnp.arange(n_col, dtype=jnp.int32)[:, None]) & is_live[None, :]
        chosen = chosen.astype(jnp.float32)
        earlier = (slot_index[:, None] < slot_index[None, :]).astype(jnp.float32)
        rank = jnp.dot(chosen, earlier)
        own_rank = jnp.sum(chosen * rank, axis=0).astype(jnp.int32)
        out_slot = jnp.clip(mode1_column[:, 0], 0, n_col - 1) * SLOTS + own_rank
        source = jnp.clip(mode2_row[:, 0], 0, n_row - 1)
        shift = (row_index // 2 - source // 2 + n_z) % n_z
        place_of = [0] * n_z
        for at, each in enumerate([0] + near):
            place_of[each] = at
        for at, each in enumerate(far):
            place_of[each] = at
        place = sum(jnp.where(shift == each, place_of[each], 0) for each in range(n_z))
        is_far = ((shift > 2) & (shift < n_z - 2)).astype(jnp.int32)
        is_other = (source % 2 != row_index % 2).astype(jnp.int32)
        table = jnp.stack(
            [
                place * JB_DEV + jnp.clip(mode2_offset, 0, JB_DEV - 1),
                jnp.clip(mode3_offset, 0, mode3_factor.shape[0] // tile_edge - 1),
                out_slot,
                is_far + 2 * is_other,
            ]
        ).astype(jnp.int32)
        slots = jnp.arange(SLOTS, dtype=jnp.float32)
        taken = chosen[:, None, :] * (rank[:, None, :] == slots[None, :, None])
        targets = jnp.sum(taken * (mode1_offset + 1).astype(jnp.float32), axis=2) - 1.0
        target_rows = jnp.zeros((8, rank_width), jnp.float32).at[0, : n_col * SLOTS].set(targets.reshape(-1))

    with jax.named_scope("normal"):
        strips = [gram_of(each).reshape(n_col, part, rank_width) for each in (mode2_factor, mode3_factor)]
        strips = lax.all_to_all(jnp.concatenate(strips, axis=1), "col", 0, 0)
        strips = jnp.sum(strips, axis=0)
        second_strips = lax.all_to_all(
            jnp.broadcast_to(strips[None, :part], (n_row, part, rank_width)), "row", 0, 0
        )
        normal_part = jnp.sum(second_strips, axis=0) * strips[part:]
        sent = jnp.concatenate([normal_part, target_rows], axis=0)
        spread = lax.all_to_all(jnp.broadcast_to(sent[None], (n_col,) + sent.shape), "col", 0, 0)
        normal_matrix = spread[:, :part].reshape(rank_width, rank_width)
        received_targets = lax.dynamic_slice_in_dim(spread[:, part], col_index * SLOTS, SLOTS, 1)
        received_targets = received_targets.astype(jnp.int32).reshape(-1)

    with jax.named_scope("contract"):
        def blocks(array):
            return array.reshape(-1, tile_edge, rank_width)

        partials = contract_tiles(
            table,
            tile_count,
            tile_values,
            blocks(mode3_factor),
            [blocks(near_own), blocks(far_own), blocks(near_other), blocks(far_other)],
            n_col * SLOTS,
        )
    with jax.named_scope("exchange"):
        received = lax.all_to_all(
            partials.reshape(n_col, SLOTS * tile_edge, rank_width), "col", 0, 0
        ).reshape(n_col * SLOTS, tile_edge, rank_width)

    with jax.named_scope("inverse"):
        inverse = invert(normal_matrix)

    with jax.named_scope("combine"):
        return combine(received_targets, received, inverse)


def solution(mesh):
    placed = (
        P(("row", "col"), None, None),
        P(("row", "col")),
        P(("row", "col"), None),
        P(("row", "col")),
        P(("row", "col"), None),
        P(("row", "col")),
        P(("row", "col")),
        P(("row", "col"), None),
        P("col", None),
    )
    return jax.shard_map(
        local, mesh=mesh, in_specs=placed, out_specs=P(("row", "col"), None), check_vma=False
    )
```

```python
import functools

import jax
import jax.numpy as jnp
from jax import lax
from jax.experimental import pallas as pl
from jax.experimental.pallas import tpu as pltpu
from jax.sharding import PartitionSpec as P

IB_DEV = 16
JB_DEV = 8
SLOTS = 4
GROUP = 4
AHEAD = 2

HIGHEST = lax.Precision.HIGHEST


def gram_of(matrix):
    return lax.dot_general(
        matrix, matrix, (((0,), (0,)), ((), ())), precision=HIGHEST, preferred_element_type=jnp.float32
    )


def split(value):
    high = value.astype(jnp.bfloat16)
    low = (value - high.astype(jnp.float32)).astype(jnp.bfloat16)
    return high, low


def dot32(left, right):
    return jnp.dot(left, right, preferred_element_type=jnp.float32)


def contract_kernel(part, table_ref, tile_hbm, third_hbm, own_hbm, other_hbm, *rest):
    out_hbm, third_buf, tile_buf, second_buf, result_buf, third_sem, tile_sem, second_sem, result_sem = rest[-9:]
    first = table_ref[5, part]
    count = table_ref[5, part + 1] - first
    groups = (count + GROUP - 1) // GROUP
    slot_count, tile_edge, depth = tile_hbm.shape
    chunk = min(256, depth)
    per_chunk = chunk // tile_edge

    def entry(row, slot):
        return table_ref[row, jnp.minimum(first + slot, slot_count - 1)]

    def third_copy():
        return pltpu.make_async_copy(third_hbm, third_buf, third_sem)

    def tile_copy(slot):
        return pltpu.make_async_copy(tile_hbm.at[entry(3, slot)], tile_buf.at[slot], tile_sem.at[slot])

    def second_copy(source, slot):
        block = jnp.minimum(entry(0, slot), source.shape[0] - 1)
        return pltpu.make_async_copy(source.at[block], second_buf.at[slot], second_sem.at[slot])

    def result_copy(slot):
        return pltpu.make_async_copy(result_buf.at[slot], out_hbm.at[entry(2, slot)], result_sem.at[slot])

    def start(group):
        for at in range(GROUP):
            slot = group * GROUP + at
            tile_copy(slot).start()
            other = entry(4, slot)

            @pl.when(other == 0)
            def _():
                second_copy(own_hbm, slot).start()

            @pl.when(other != 0)
            def _():
                second_copy(other_hbm, slot).start()

    third_copy().start()
    for group in range(AHEAD):

        @pl.when(group < groups)
        def _():
            start(group)

    third_copy().wait()

    def contract(group, carry):
        @pl.when(group + AHEAD < groups)
        def _():
            start(group + AHEAD)

        for at in range(GROUP):
            tile_copy(group * GROUP + at).wait()
            second_copy(own_hbm, group * GROUP + at).wait()
        for at in range(GROUP):
            slot = group * GROUP + at
            second = second_buf[slot]
            third = third_buf[entry(1, slot)]
            high, low = split(tile_buf[slot])
            both = jnp.concatenate([high, low], axis=0)
            total = jnp.zeros((2 * tile_edge, third.shape[1]), jnp.float32)
            total_low = jnp.zeros((tile_edge, third.shape[1]), jnp.float32)
            for q in range(depth // chunk):
                rows = second[q * per_chunk : (q + 1) * per_chunk]
                khatri = (rows[:, None, :] * third[None, :, :]).reshape(chunk, third.shape[1])
                khatri_high, khatri_low = split(khatri)
                total = total + dot32(both[:, q * chunk : (q + 1) * chunk], khatri_high)
                total_low = total_low + dot32(high[:, q * chunk : (q + 1) * chunk], khatri_low)
            result_buf[slot] = total[:tile_edge] + (total[tile_edge:] + total_low)
        for at in range(GROUP):
            slot = group * GROUP + at

            @pl.when(slot < count)
            def _():
                result_copy(slot).start()

        return carry

    lax.fori_loop(0, groups, contract, 0)

    def finish(slot, carry):
        result_copy(slot).wait()
        return carry

    lax.fori_loop(0, count, finish, 0)


def contract_tiles(part, table, tile_values, third_blocks, sources, out_slots, earlier=()):
    slot_count, tile_edge, depth = tile_values.shape
    rank_width = third_blocks.shape[2]
    hbm = pl.BlockSpec(memory_space=pltpu.HBM)
    block = (slot_count, tile_edge, rank_width)
    return pl.pallas_call(
        functools.partial(contract_kernel, part),
        out_shape=jax.ShapeDtypeStruct((out_slots, tile_edge, rank_width), jnp.float32),
        in_specs=[pl.BlockSpec(memory_space=pltpu.SMEM)] + [hbm] * (4 + len(earlier)),
        out_specs=hbm,
        scratch_shapes=[
            pltpu.VMEM(third_blocks.shape, jnp.float32),
            pltpu.VMEM((slot_count, tile_edge, depth), jnp.float32),
            pltpu.VMEM(block, jnp.float32),
            pltpu.VMEM(block, jnp.float32),
            pltpu.SemaphoreType.DMA,
            pltpu.SemaphoreType.DMA((slot_count,)),
            pltpu.SemaphoreType.DMA((slot_count,)),
            pltpu.SemaphoreType.DMA((slot_count,)),
        ],
        input_output_aliases={5: 0} if earlier else {},
        compiler_params=pltpu.CompilerParams(vmem_limit_bytes=60 * 1024 * 1024),
        cost_estimate=pl.CostEstimate(
            flops=3 * slot_count * tile_edge * depth * rank_width, bytes_accessed=5_000_000, transcendentals=0
        ),
        name="contract",
    )(table, tile_values, third_blocks, *sources, *earlier)


def combine_kernel(target_ref, received_ref, inverse_ref, out_ref, total_ref):
    slot_count, tile_edge, _ = received_ref.shape
    total_ref[...] = jnp.zeros_like(total_ref)

    def add(step, carry):
        for at in range(8):
            slot = step * 8 + at
            target = target_ref[slot]
            rows = pl.ds(pl.multiple_of(jnp.maximum(target, 0) * tile_edge, tile_edge), tile_edge)

            @pl.when(target >= 0)
            def _():
                total_ref[rows, :] += received_ref[slot]

        return carry

    lax.fori_loop(0, slot_count // 8, add, 0)
    high, low = split(total_ref[...])
    inverse_high, inverse_low = split(inverse_ref[...])
    out_ref[...] = dot32(high, inverse_high) + (dot32(low, inverse_high) + dot32(high, inverse_low))


def combine(targets, received, inverse):
    tile_edge, rank_width = received.shape[1:]
    vmem = pl.BlockSpec(memory_space=pltpu.VMEM)
    return pl.pallas_call(
        combine_kernel,
        out_shape=jax.ShapeDtypeStruct((IB_DEV * tile_edge, rank_width), jnp.float32),
        in_specs=[pl.BlockSpec(memory_space=pltpu.SMEM), vmem, vmem],
        out_specs=vmem,
        scratch_shapes=[pltpu.VMEM((IB_DEV * tile_edge, rank_width), jnp.float32)],
        compiler_params=pltpu.CompilerParams(vmem_limit_bytes=16 * 1024 * 1024),
        name="combine",
    )(targets, received, inverse)


def invert_four(s):
    det = s[0][0] * s[1][1] - s[0][1] * s[0][1]
    over = 1.0 / det
    a00, a01, a11 = s[1][1] * over, -s[0][1] * over, s[0][0] * over
    y00 = a00 * s[0][2] + a01 * s[1][2]
    y01 = a00 * s[0][3] + a01 * s[1][3]
    y10 = a01 * s[0][2] + a11 * s[1][2]
    y11 = a01 * s[0][3] + a11 * s[1][3]
    c00 = s[2][2] - (s[0][2] * y00 + s[1][2] * y10)
    c01 = s[2][3] - (s[0][2] * y01 + s[1][2] * y11)
    c11 = s[3][3] - (s[0][3] * y01 + s[1][3] * y11)
    over = 1.0 / (c00 * c11 - c01 * c01)
    d00, d01, d11 = c11 * over, -c01 * over, c00 * over
    e00 = -(y00 * d00 + y01 * d01)
    e01 = -(y00 * d01 + y01 * d11)
    e10 = -(y10 * d00 + y11 * d01)
    e11 = -(y10 * d01 + y11 * d11)
    b00 = a00 - (e00 * y00 + e01 * y01)
    b01 = a01 - (e00 * y10 + e01 * y11)
    b11 = a11 - (e10 * y10 + e11 * y11)
    return [[b00, b01, e00, e01], [b01, b11, e10, e11], [e00, e10, d00, d01], [e01, e11, d01, d11]]

def invert_block(groups):
    width = groups[0].shape[1]
    full = (8, width)
    lane = lax.broadcasted_iota(jnp.int32, full, 1)
    sub = lax.broadcasted_iota(jnp.int32, full, 0)
    for first in range(0, width, 4):
        at, off = first // 8, first % 8
        cols = [[jnp.broadcast_to(g[:, first + j : first + j + 1], full) for j in range(4)] for g in groups]
        s = [[jnp.broadcast_to(cols[at][j][off + i : off + i + 1], full) if i <= j else None for j in range(4)] for i in range(4)]
        rows = [jnp.broadcast_to(groups[at][off + i : off + i + 1], full) for i in range(4)]
        d = invert_four(s)
        new_rows = []
        for i in range(4):
            w = d[i][0] * rows[0] + d[i][1] * rows[1] + d[i][2] * rows[2] + d[i][3] * rows[3]
            for j in range(4):
                w = jnp.where(lane == first + j, d[i][j], w)
            new_rows.append(w)
        in_pivot = (lane >= first) & (lane < first + 4)
        out = []
        for k, g in enumerate(groups):
            v = jnp.where(in_pivot, 0.0, g)
            v = v - ((cols[k][0] * new_rows[0] + cols[k][1] * new_rows[1]) + (cols[k][2] * new_rows[2] + cols[k][3] * new_rows[3]))
            if k == at:
                for i in range(4):
                    v = jnp.where(sub == off + i, new_rows[i], v)
            out.append(v)
        groups = out
    return groups

def invert_kernel(block, normal_ref, out_ref, work_ref):
    n = normal_ref.shape[0]
    normal = normal_ref[...]
    on_diagonal = lax.broadcasted_iota(jnp.int32, (n, n), 0) == lax.broadcasted_iota(jnp.int32, (n, n), 1)
    diagonal = jnp.where(on_diagonal, normal, 0.0)
    scale_row = lax.rsqrt(jnp.sum(diagonal, axis=0, keepdims=True))
    scale_col = lax.rsqrt(jnp.sum(diagonal, axis=1, keepdims=True))
    work_ref[...] = normal * scale_col * scale_row
    for first in range(0, n, block):
        last = first + block
        groups = [work_ref[r : r + 8, first:last] for r in range(first, last, 8)]
        inner = jnp.concatenate(invert_block(groups), axis=0)
        rows = jnp.dot(inner, work_ref[first:last, :], precision=HIGHEST, preferred_element_type=jnp.float32)
        pieces = [rows[:, :first]] if first else []
        pieces.append(inner)
        if last < n:
            pieces.append(rows[:, last:])
        rows = jnp.concatenate(pieces, axis=1)
        change = jnp.dot(work_ref[:, first:last], rows, precision=HIGHEST, preferred_element_type=jnp.float32)
        lane = lax.broadcasted_iota(jnp.int32, (n, n), 1)
        work_ref[...] = jnp.where((lane >= first) & (lane < last), 0.0, work_ref[...]) - change
        work_ref[first:last, :] = rows
    out_ref[...] = work_ref[...] * scale_col * scale_row

def invert(normal, block=64):
    n = normal.shape[0]
    vmem = pl.BlockSpec(memory_space=pltpu.VMEM)
    return pl.pallas_call(
        functools.partial(invert_kernel, block),
        out_shape=jax.ShapeDtypeStruct((n, n), jnp.float32),
        in_specs=[vmem], out_specs=vmem,
        scratch_shapes=[pltpu.VMEM((n, n), jnp.float32)],
        compiler_params=pltpu.CompilerParams(vmem_limit_bytes=16 * 1024 * 1024),
        cost_estimate=pl.CostEstimate(flops=12 * n * n * n, bytes_accessed=8 * n * n, transcendentals=0),
        name="invert",
    )(normal)


def local(
    tile_values,
    tile_count,
    mode1_column,
    mode1_offset,
    mode2_row,
    mode2_offset,
    mode3_offset,
    mode2_factor,
    mode3_factor,
):
    slot_count, tile_edge, _ = tile_values.shape
    rank_width = mode2_factor.shape[1]
    row_index = lax.axis_index("row")
    col_index = lax.axis_index("col")
    n_row = lax.axis_size("row")
    n_col = lax.axis_size("col")
    part = rank_width // n_col

    with jax.named_scope("gather_second"):
        n_z = n_row // 2

        def moved(array, shift):
            pairs = [(i, 2 * ((i // 2 + shift) % n_z) + i % 2) for i in range(n_row)]
            return lax.ppermute(array, "row", pairs)

        near = [1, n_z - 1, 2, n_z - 2]
        far = [3, n_z - 3, 4]
        twin = [(i, i ^ 1) for i in range(n_row)]
        up_1, down_1 = moved(mode2_factor, 1), moved(mode2_factor, -1)
        up_2, down_2 = moved(up_1, 1), moved(down_1, -1)
        up_3, down_3 = moved(up_2, 1), moved(down_2, -1)
        middle = mode2_factor.shape[0] // 2
        up_4, down_4 = moved(up_3[:middle], 1), moved(down_3[middle:], -1)
        near_own = jnp.concatenate([mode2_factor, up_1, down_1, up_2, down_2], axis=0)
        near_other = lax.ppermute(near_own, "row", twin)

    with jax.named_scope("tables"):
        slot_index = jnp.arange(slot_count, dtype=jnp.int32)
        is_live = slot_index < tile_count[0]
        chosen = (mode1_column[:, 0][None, :] == jnp.arange(n_col, dtype=jnp.int32)[:, None]) & is_live[None, :]
        chosen = chosen.astype(jnp.float32)
        earlier = (slot_index[:, None] < slot_index[None, :]).astype(jnp.float32)
        rank = jnp.dot(chosen, earlier)
        own_rank = jnp.sum(chosen * rank, axis=0).astype(jnp.int32)
        out_slot = jnp.clip(mode1_column[:, 0], 0, n_col - 1) * SLOTS + own_rank
        source = jnp.clip(mode2_row[:, 0], 0, n_row - 1)
        shift = (row_index // 2 - source // 2 + n_z) % n_z
        place_of = [0] * n_z
        for at, each in enumerate([0] + near):
            place_of[each] = at
        for at, each in enumerate(far):
            place_of[each] = at
        place = sum(jnp.where(shift == each, place_of[each], 0) for each in range(n_z))
        is_far = ((shift > 2) & (shift < n_z - 2)).astype(jnp.int32)
        is_other = (source % 2 != row_index % 2).astype(jnp.int32)
        table = jnp.stack(
            [
                place * JB_DEV + jnp.clip(mode2_offset, 0, JB_DEV - 1),
                jnp.clip(mode3_offset, 0, mode3_factor.shape[0] // tile_edge - 1),
                out_slot,
                slot_index,
                is_other,
            ]
        ).astype(jnp.float32)
        group = jnp.where(is_live, is_far, 2)
        ahead = (group[:, None] < group[None, :]) | (
            (group[:, None] == group[None, :]) & (slot_index[:, None] < slot_index[None, :])
        )
        position = jnp.sum(ahead.astype(jnp.int32), axis=0)
        placed = (position[:, None] == slot_index[None, :]).astype(jnp.float32)
        near_count = jnp.sum((group == 0).astype(jnp.int32))
        bounds = jnp.where(slot_index == 1, near_count, jnp.where(slot_index == 2, tile_count[0], 0))
        table = jnp.dot(table, placed, precision=HIGHEST)
        table = jnp.concatenate([table.astype(jnp.int32), bounds[None, :]], axis=0)
        slots = jnp.arange(SLOTS, dtype=jnp.float32)
        taken = chosen[:, None, :] * (rank[:, None, :] == slots[None, :, None])
        targets = jnp.sum(taken * (mode1_offset + 1).astype(jnp.float32), axis=2) - 1.0
        target_rows = jnp.zeros((8, rank_width), jnp.float32).at[0, : n_col * SLOTS].set(targets.reshape(-1))

    def blocks(array):
        return array.reshape(-1, tile_edge, rank_width)

    with jax.named_scope("contract"):
        near_partials = contract_tiles(
            0, table, tile_values, blocks(mode3_factor), [blocks(near_own), blocks(near_other)], n_col * SLOTS
        )
    with jax.named_scope("gather_far"):
        up_4, down_4, near_partials = lax.optimization_barrier((up_4, down_4, near_partials))
        far_own = jnp.concatenate([up_3, down_3, up_4, down_4], axis=0)
        far_other = lax.ppermute(far_own, "row", twin)

    with jax.named_scope("normal"):
        strips = [gram_of(each).reshape(n_col, part, rank_width) for each in (mode2_factor, mode3_factor)]
        strips = lax.all_to_all(jnp.concatenate(strips, axis=1), "col", 0, 0)
        strips = jnp.sum(strips, axis=0)
        second_strips = lax.all_to_all(
            jnp.broadcast_to(strips[None, :part], (n_row, part, rank_width)), "row", 0, 0
        )
        normal_part = jnp.sum(second_strips, axis=0) * strips[part:]
        sent = jnp.concatenate([normal_part, target_rows], axis=0)
        spread = lax.all_to_all(jnp.broadcast_to(sent[None], (n_col,) + sent.shape), "col", 0, 0)
        normal_matrix = spread[:, :part].reshape(rank_width, rank_width)
        received_targets = lax.dynamic_slice_in_dim(spread[:, part], col_index * SLOTS, SLOTS, 1)
        received_targets = received_targets.astype(jnp.int32).reshape(-1)

    with jax.named_scope("contract"):
        partials = contract_tiles(
            1,
            table,
            tile_values,
            blocks(mode3_factor),
            [blocks(far_own), blocks(far_other)],
            n_col * SLOTS,
            (near_partials,),
        )
    with jax.named_scope("exchange"):
        received = lax.all_to_all(
            partials.reshape(n_col, SLOTS * tile_edge, rank_width), "col", 0, 0
        ).reshape(n_col * SLOTS, tile_edge, rank_width)

    with jax.named_scope("inverse"):
        inverse = invert(normal_matrix)

    with jax.named_scope("combine"):
        return combine(received_targets, received, inverse)


def solution(mesh):
    placed = (
        P(("row", "col"), None, None),
        P(("row", "col")),
        P(("row", "col"), None),
        P(("row", "col")),
        P(("row", "col"), None),
        P(("row", "col")),
        P(("row", "col")),
        P(("row", "col"), None),
        P("col", None),
    )
    return jax.shard_map(
        local, mesh=mesh, in_specs=placed, out_specs=P(("row", "col"), None), check_vma=False
    )
```

```python
import functools

import jax
import jax.numpy as jnp
from jax import lax
from jax.experimental import pallas as pl
from jax.experimental.pallas import tpu as pltpu
from jax.sharding import PartitionSpec as P

IB_DEV = 16
JB_DEV = 8
SLOTS = 4
GROUP = 4
AHEAD = 2

HIGHEST = lax.Precision.HIGHEST


def gram_of(matrix):
    return lax.dot_general(
        matrix, matrix, (((0,), (0,)), ((), ())), precision=HIGHEST, preferred_element_type=jnp.float32
    )


def split(value):
    high = value.astype(jnp.bfloat16)
    low = (value - high.astype(jnp.float32)).astype(jnp.bfloat16)
    return high, low


def dot32(left, right):
    return jnp.dot(left, right, preferred_element_type=jnp.float32)


def contract_kernel(table_ref, count_ref, tile_hbm, third_ref, *rest):
    sources, rest = rest[:-7], rest[-7:]
    out_hbm, tile_buf, second_buf, result_buf, tile_sem, second_sem, result_sem = rest
    count = count_ref[0]
    groups = (count + GROUP - 1) // GROUP
    slot_count, tile_edge, depth = tile_hbm.shape
    chunk = min(256, depth)
    per_chunk = chunk // tile_edge

    def tile_copy(group):
        span = pl.ds(group * GROUP, GROUP)
        return pltpu.make_async_copy(tile_hbm.at[span], tile_buf.at[span], tile_sem.at[group])

    def second_copy(source, slot):
        return pltpu.make_async_copy(source.at[table_ref[0, slot]], second_buf.at[slot], second_sem.at[slot])

    def result_copy(slot):
        return pltpu.make_async_copy(result_buf.at[slot], out_hbm.at[table_ref[2, slot]], result_sem.at[slot])

    def start(group):
        tile_copy(group).start()
        for at in range(GROUP):
            slot = group * GROUP + at
            if len(sources) == 1:
                second_copy(sources[0], slot).start()
            else:
                chosen = table_ref[3, slot]
                for which, source in enumerate(sources):

                    @pl.when(chosen == which)
                    def _():
                        second_copy(source, slot).start()

    for group in range(AHEAD):

        @pl.when(group < groups)
        def _():
            start(group)

    def contract(group, carry):
        @pl.when(group + AHEAD < groups)
        def _():
            start(group + AHEAD)

        tile_copy(group).wait()
        for at in range(GROUP):
            second_copy(sources[0], group * GROUP + at).wait()
        for at in range(GROUP):
            slot = group * GROUP + at
            second = second_buf[slot]
            third = third_ref[table_ref[1, slot]]
            high, low = split(tile_buf[slot])
            both = jnp.concatenate([high, low], axis=0)
            total = jnp.zeros((2 * tile_edge, third.shape[1]), jnp.float32)
            total_low = jnp.zeros((tile_edge, third.shape[1]), jnp.float32)
            for q in range(depth // chunk):
                rows = second[q * per_chunk : (q + 1) * per_chunk]
                khatri = (rows[:, None, :] * third[None, :, :]).reshape(chunk, third.shape[1])
                khatri_high, khatri_low = split(khatri)
                total = total + dot32(both[:, q * chunk : (q + 1) * chunk], khatri_high)
                total_low = total_low + dot32(high[:, q * chunk : (q + 1) * chunk], khatri_low)
            result_buf[slot] = total[:tile_edge] + (total[tile_edge:] + total_low)
        for at in range(GROUP):
            slot = group * GROUP + at

            @pl.when(slot < count)
            def _():
                result_copy(slot).start()

        return carry

    lax.fori_loop(0, groups, contract, 0)

    def finish(slot, carry):
        result_copy(slot).wait()
        return carry

    lax.fori_loop(0, count, finish, 0)


def contract_tiles(table, count, tile_values, third_blocks, sources, out_slots):
    slot_count, tile_edge, depth = tile_values.shape
    rank_width = third_blocks.shape[2]
    smem = pl.BlockSpec(memory_space=pltpu.SMEM)
    vmem = pl.BlockSpec(memory_space=pltpu.VMEM)
    hbm = pl.BlockSpec(memory_space=pltpu.HBM)
    block = (slot_count, tile_edge, rank_width)
    return pl.pallas_call(
        contract_kernel,
        out_shape=jax.ShapeDtypeStruct((out_slots, tile_edge, rank_width), jnp.float32),
        in_specs=[smem, smem, hbm, vmem] + [hbm] * len(sources),
        out_specs=hbm,
        scratch_shapes=[
            pltpu.VMEM((slot_count, tile_edge, depth), jnp.float32),
            pltpu.VMEM(block, jnp.float32),
            pltpu.VMEM(block, jnp.float32),
            pltpu.SemaphoreType.DMA((slot_count // GROUP,)),
            pltpu.SemaphoreType.DMA((slot_count,)),
            pltpu.SemaphoreType.DMA((slot_count,)),
        ],
        compiler_params=pltpu.CompilerParams(vmem_limit_bytes=60 * 1024 * 1024),
        cost_estimate=pl.CostEstimate(
            flops=6 * slot_count * tile_edge * depth * rank_width, bytes_accessed=10_000_000, transcendentals=0
        ),
        name="contract",
    )(table, count, tile_values, third_blocks, *sources)


def combine_kernel(target_ref, received_ref, inverse_ref, out_ref, total_ref):
    slot_count, tile_edge, _ = received_ref.shape
    total_ref[...] = jnp.zeros_like(total_ref)

    def add(step, carry):
        for at in range(8):
            slot = step * 8 + at
            target = target_ref[slot]
            rows = pl.ds(pl.multiple_of(jnp.maximum(target, 0) * tile_edge, tile_edge), tile_edge)

            @pl.when(target >= 0)
            def _():
                total_ref[rows, :] += received_ref[slot]

        return carry

    lax.fori_loop(0, slot_count // 8, add, 0)
    high, low = split(total_ref[...])
    inverse_high, inverse_low = split(inverse_ref[...])
    out_ref[...] = dot32(high, inverse_high) + (dot32(low, inverse_high) + dot32(high, inverse_low))


def combine(targets, received, inverse):
    tile_edge, rank_width = received.shape[1:]
    vmem = pl.BlockSpec(memory_space=pltpu.VMEM)
    return pl.pallas_call(
        combine_kernel,
        out_shape=jax.ShapeDtypeStruct((IB_DEV * tile_edge, rank_width), jnp.float32),
        in_specs=[pl.BlockSpec(memory_space=pltpu.SMEM), vmem, vmem],
        out_specs=vmem,
        scratch_shapes=[pltpu.VMEM((IB_DEV * tile_edge, rank_width), jnp.float32)],
        compiler_params=pltpu.CompilerParams(vmem_limit_bytes=16 * 1024 * 1024),
        name="combine",
    )(targets, received, inverse)


def invert_four(s):
    det = s[0][0] * s[1][1] - s[0][1] * s[0][1]
    over = 1.0 / det
    a00, a01, a11 = s[1][1] * over, -s[0][1] * over, s[0][0] * over
    y00 = a00 * s[0][2] + a01 * s[1][2]
    y01 = a00 * s[0][3] + a01 * s[1][3]
    y10 = a01 * s[0][2] + a11 * s[1][2]
    y11 = a01 * s[0][3] + a11 * s[1][3]
    c00 = s[2][2] - (s[0][2] * y00 + s[1][2] * y10)
    c01 = s[2][3] - (s[0][2] * y01 + s[1][2] * y11)
    c11 = s[3][3] - (s[0][3] * y01 + s[1][3] * y11)
    over = 1.0 / (c00 * c11 - c01 * c01)
    d00, d01, d11 = c11 * over, -c01 * over, c00 * over
    e00 = -(y00 * d00 + y01 * d01)
    e01 = -(y00 * d01 + y01 * d11)
    e10 = -(y10 * d00 + y11 * d01)
    e11 = -(y10 * d01 + y11 * d11)
    b00 = a00 - (e00 * y00 + e01 * y01)
    b01 = a01 - (e00 * y10 + e01 * y11)
    b11 = a11 - (e10 * y10 + e11 * y11)
    return [[b00, b01, e00, e01], [b01, b11, e10, e11], [e00, e10, d00, d01], [e01, e11, d01, d11]]

def invert_block(groups):
    width = groups[0].shape[1]
    full = (8, width)
    lane = lax.broadcasted_iota(jnp.int32, full, 1)
    sub = lax.broadcasted_iota(jnp.int32, full, 0)
    for first in range(0, width, 4):
        at, off = first // 8, first % 8
        cols = [[jnp.broadcast_to(g[:, first + j : first + j + 1], full) for j in range(4)] for g in groups]
        s = [[jnp.broadcast_to(cols[at][j][off + i : off + i + 1], full) if i <= j else None for j in range(4)] for i in range(4)]
        rows = [jnp.broadcast_to(groups[at][off + i : off + i + 1], full) for i in range(4)]
        d = invert_four(s)
        new_rows = []
        for i in range(4):
            w = d[i][0] * rows[0] + d[i][1] * rows[1] + d[i][2] * rows[2] + d[i][3] * rows[3]
            for j in range(4):
                w = jnp.where(lane == first + j, d[i][j], w)
            new_rows.append(w)
        in_pivot = (lane >= first) & (lane < first + 4)
        out = []
        for k, g in enumerate(groups):
            v = jnp.where(in_pivot, 0.0, g)
            v = v - ((cols[k][0] * new_rows[0] + cols[k][1] * new_rows[1]) + (cols[k][2] * new_rows[2] + cols[k][3] * new_rows[3]))
            if k == at:
                for i in range(4):
                    v = jnp.where(sub == off + i, new_rows[i], v)
            out.append(v)
        groups = out
    return groups

def invert_kernel(block, normal_ref, out_ref, work_ref):
    n = normal_ref.shape[0]
    normal = normal_ref[...]
    on_diagonal = lax.broadcasted_iota(jnp.int32, (n, n), 0) == lax.broadcasted_iota(jnp.int32, (n, n), 1)
    diagonal = jnp.where(on_diagonal, normal, 0.0)
    scale_row = lax.rsqrt(jnp.sum(diagonal, axis=0, keepdims=True))
    scale_col = lax.rsqrt(jnp.sum(diagonal, axis=1, keepdims=True))
    work_ref[...] = normal * scale_col * scale_row
    for first in range(0, n, block):
        last = first + block
        groups = [work_ref[r : r + 8, first:last] for r in range(first, last, 8)]
        inner = jnp.concatenate(invert_block(groups), axis=0)
        rows = jnp.dot(inner, work_ref[first:last, :], precision=HIGHEST, preferred_element_type=jnp.float32)
        pieces = [rows[:, :first]] if first else []
        pieces.append(inner)
        if last < n:
            pieces.append(rows[:, last:])
        rows = jnp.concatenate(pieces, axis=1)
        change = jnp.dot(work_ref[:, first:last], rows, precision=HIGHEST, preferred_element_type=jnp.float32)
        lane = lax.broadcasted_iota(jnp.int32, (n, n), 1)
        work_ref[...] = jnp.where((lane >= first) & (lane < last), 0.0, work_ref[...]) - change
        work_ref[first:last, :] = rows
    out_ref[...] = work_ref[...] * scale_col * scale_row

def invert(normal, block=64):
    n = normal.shape[0]
    vmem = pl.BlockSpec(memory_space=pltpu.VMEM)
    return pl.pallas_call(
        functools.partial(invert_kernel, block),
        out_shape=jax.ShapeDtypeStruct((n, n), jnp.float32),
        in_specs=[vmem], out_specs=vmem,
        scratch_shapes=[pltpu.VMEM((n, n), jnp.float32)],
        compiler_params=pltpu.CompilerParams(vmem_limit_bytes=16 * 1024 * 1024),
        cost_estimate=pl.CostEstimate(flops=12 * n * n * n, bytes_accessed=8 * n * n, transcendentals=0),
        name="invert",
    )(normal)


def local(
    tile_values,
    tile_count,
    mode1_column,
    mode1_offset,
    mode2_row,
    mode2_offset,
    mode3_offset,
    mode2_factor,
    mode3_factor,
):
    slot_count, tile_edge, _ = tile_values.shape
    rank_width = mode2_factor.shape[1]
    row_index = lax.axis_index("row")
    col_index = lax.axis_index("col")
    n_row = lax.axis_size("row")
    n_col = lax.axis_size("col")
    part = rank_width // n_col

    with jax.named_scope("normal"):
        strips = [gram_of(each).reshape(n_col, part, rank_width) for each in (mode2_factor, mode3_factor)]
        strips = jnp.concatenate(strips, axis=1)
        held_second, strips = lax.optimization_barrier((mode2_factor, strips))
        strips = lax.all_to_all(strips, "col", 0, 0)

    with jax.named_scope("gather_second"):
        n_z = n_row // 2

        def moved(array, shift):
            pairs = [(i, 2 * ((i // 2 + shift) % n_z) + i % 2) for i in range(n_row)]
            return lax.ppermute(array, "row", pairs)

        near = [1, n_z - 1, 2, n_z - 2]
        far = [3, n_z - 3, 4]
        twin = [(i, i ^ 1) for i in range(n_row)]
        up_1, down_1 = moved(held_second, 1), moved(held_second, -1)
        across = moved(held_second, n_z // 2)
        up_2, down_2 = moved(up_1, 1), moved(down_1, -1)
        up_3, down_3 = moved(up_2, 1), moved(down_2, -1)
        near_own = jnp.concatenate([mode2_factor, up_1, down_1, up_2, down_2], axis=0)
        far_own = jnp.concatenate([up_3, down_3, across], axis=0)
        near_other = lax.ppermute(near_own, "row", twin)
        far_other = lax.ppermute(far_own, "row", twin)

    with jax.named_scope("tables"):
        slot_index = jnp.arange(slot_count, dtype=jnp.int32)
        is_live = slot_index < tile_count[0]
        chosen = (mode1_column[:, 0][None, :] == jnp.arange(n_col, dtype=jnp.int32)[:, None]) & is_live[None, :]
        chosen = chosen.astype(jnp.float32)
        earlier = (slot_index[:, None] < slot_index[None, :]).astype(jnp.float32)
        rank = jnp.dot(chosen, earlier)
        own_rank = jnp.sum(chosen * rank, axis=0).astype(jnp.int32)
        out_slot = jnp.clip(mode1_column[:, 0], 0, n_col - 1) * SLOTS + own_rank
        source = jnp.clip(mode2_row[:, 0], 0, n_row - 1)
        shift = (row_index // 2 - source // 2 + n_z) % n_z
        place_of = [0] * n_z
        for at, each in enumerate([0] + near):
            place_of[each] = at
        for at, each in enumerate(far):
            place_of[each] = at
        place = sum(jnp.where(shift == each, place_of[each], 0) for each in range(n_z))
        is_far = ((shift > 2) & (shift < n_z - 2)).astype(jnp.int32)
        is_other = (source % 2 != row_index % 2).astype(jnp.int32)
        table = jnp.stack(
            [
                place * JB_DEV + jnp.clip(mode2_offset, 0, JB_DEV - 1),
                jnp.clip(mode3_offset, 0, mode3_factor.shape[0] // tile_edge - 1),
                out_slot,
                is_far + 2 * is_other,
            ]
        ).astype(jnp.int32)
        slots = jnp.arange(SLOTS, dtype=jnp.float32)
        taken = chosen[:, None, :] * (rank[:, None, :] == slots[None, :, None])
        targets = jnp.sum(taken * (mode1_offset + 1).astype(jnp.float32), axis=2) - 1.0
        target_rows = jnp.zeros((8, rank_width), jnp.float32).at[0, : n_col * SLOTS].set(targets.reshape(-1))

    with jax.named_scope("normal"):
        strips = jnp.sum(strips, axis=0)
        second_strips = lax.all_to_all(
            jnp.broadcast_to(strips[None, :part], (n_row, part, rank_width)), "row", 0, 0
        )
        normal_part = jnp.sum(second_strips, axis=0) * strips[part:]
        sent = jnp.concatenate([normal_part, target_rows], axis=0)
        spread = lax.all_to_all(jnp.broadcast_to(sent[None], (n_col,) + sent.shape), "col", 0, 0)
        normal_matrix = spread[:, :part].reshape(rank_width, rank_width)
        received_targets = lax.dynamic_slice_in_dim(spread[:, part], col_index * SLOTS, SLOTS, 1)
        received_targets = received_targets.astype(jnp.int32).reshape(-1)

    with jax.named_scope("contract"):
        def blocks(array):
            return array.reshape(-1, tile_edge, rank_width)

        partials = contract_tiles(
            table,
            tile_count,
            tile_values,
            blocks(mode3_factor),
            [blocks(near_own), blocks(far_own), blocks(near_other), blocks(far_other)],
            n_col * SLOTS,
        )
    with jax.named_scope("exchange"):
        received = lax.all_to_all(
            partials.reshape(n_col, SLOTS * tile_edge, rank_width), "col", 0, 0
        ).reshape(n_col * SLOTS, tile_edge, rank_width)

    with jax.named_scope("inverse"):
        inverse = invert(normal_matrix)

    with jax.named_scope("combine"):
        return combine(received_targets, received, inverse)


def solution(mesh):
    placed = (
        P(("row", "col"), None, None),
        P(("row", "col")),
        P(("row", "col"), None),
        P(("row", "col")),
        P(("row", "col"), None),
        P(("row", "col")),
        P(("row", "col")),
        P(("row", "col"), None),
        P("col", None),
    )
    return jax.shard_map(
        local, mesh=mesh, in_specs=placed, out_specs=P(("row", "col"), None), check_vma=False
    )
```

```python
import functools

import jax
import jax.numpy as jnp
from jax import lax
from jax.experimental import pallas as pl
from jax.experimental.pallas import tpu as pltpu
from jax.sharding import PartitionSpec as P

IB_DEV = 16
JB_DEV = 8
SLOTS = 4
GROUP = 4
AHEAD = 2

HIGHEST = lax.Precision.HIGHEST


def gram_of(matrix):
    return lax.dot_general(
        matrix, matrix, (((0,), (0,)), ((), ())), precision=HIGHEST, preferred_element_type=jnp.float32
    )


def split(value):
    high = value.astype(jnp.bfloat16)
    low = (value - high.astype(jnp.float32)).astype(jnp.bfloat16)
    return high, low


def dot32(left, right):
    return jnp.dot(left, right, preferred_element_type=jnp.float32)


def contract_kernel(table_ref, count_ref, tile_hbm, third_ref, *rest):
    sources, rest = rest[:-7], rest[-7:]
    out_hbm, tile_buf, second_buf, result_buf, tile_sem, second_sem, result_sem = rest
    count = count_ref[0]
    groups = (count + GROUP - 1) // GROUP
    slot_count, tile_edge, depth = tile_hbm.shape
    chunk = min(256, depth)
    per_chunk = chunk // tile_edge

    def tile_copy(group):
        span = pl.ds(group * GROUP, GROUP)
        return pltpu.make_async_copy(tile_hbm.at[span], tile_buf.at[span], tile_sem.at[group])

    def second_copy(source, slot):
        return pltpu.make_async_copy(source.at[table_ref[0, slot]], second_buf.at[slot], second_sem.at[slot])

    def result_copy(slot):
        return pltpu.make_async_copy(result_buf.at[slot], out_hbm.at[table_ref[2, slot]], result_sem.at[slot])

    def start(group):
        tile_copy(group).start()
        for at in range(GROUP):
            slot = group * GROUP + at
            if len(sources) == 1:
                second_copy(sources[0], slot).start()
            else:
                chosen = table_ref[3, slot]
                for which, source in enumerate(sources):

                    @pl.when(chosen == which)
                    def _():
                        second_copy(source, slot).start()

    for group in range(AHEAD):

        @pl.when(group < groups)
        def _():
            start(group)

    def contract(group, carry):
        @pl.when(group + AHEAD < groups)
        def _():
            start(group + AHEAD)

        tile_copy(group).wait()
        for at in range(GROUP):
            second_copy(sources[0], group * GROUP + at).wait()
        for at in range(GROUP):
            slot = group * GROUP + at
            second = second_buf[slot]
            third = third_ref[table_ref[1, slot]]
            high, low = split(tile_buf[slot])
            both = jnp.concatenate([high, low], axis=0)
            total = jnp.zeros((2 * tile_edge, third.shape[1]), jnp.float32)
            total_low = jnp.zeros((tile_edge, third.shape[1]), jnp.float32)
            for q in range(depth // chunk):
                rows = second[q * per_chunk : (q + 1) * per_chunk]
                khatri = (rows[:, None, :] * third[None, :, :]).reshape(chunk, third.shape[1])
                khatri_high, khatri_low = split(khatri)
                total = total + dot32(both[:, q * chunk : (q + 1) * chunk], khatri_high)
                total_low = total_low + dot32(high[:, q * chunk : (q + 1) * chunk], khatri_low)
            result_buf[slot] = total[:tile_edge] + (total[tile_edge:] + total_low)
        for at in range(GROUP):
            slot = group * GROUP + at

            @pl.when(slot < count)
            def _():
                result_copy(slot).start()

        return carry

    lax.fori_loop(0, groups, contract, 0)

    def finish(slot, carry):
        result_copy(slot).wait()
        return carry

    lax.fori_loop(0, count, finish, 0)


def contract_tiles(table, count, tile_values, third_blocks, sources, out_slots):
    slot_count, tile_edge, depth = tile_values.shape
    rank_width = third_blocks.shape[2]
    smem = pl.BlockSpec(memory_space=pltpu.SMEM)
    vmem = pl.BlockSpec(memory_space=pltpu.VMEM)
    hbm = pl.BlockSpec(memory_space=pltpu.HBM)
    block = (slot_count, tile_edge, rank_width)
    return pl.pallas_call(
        contract_kernel,
        out_shape=jax.ShapeDtypeStruct((out_slots, tile_edge, rank_width), jnp.float32),
        in_specs=[smem, smem, hbm, vmem] + [hbm] * len(sources),
        out_specs=hbm,
        scratch_shapes=[
            pltpu.VMEM((slot_count, tile_edge, depth), jnp.float32),
            pltpu.VMEM(block, jnp.float32),
            pltpu.VMEM(block, jnp.float32),
            pltpu.SemaphoreType.DMA((slot_count // GROUP,)),
            pltpu.SemaphoreType.DMA((slot_count,)),
            pltpu.SemaphoreType.DMA((slot_count,)),
        ],
        compiler_params=pltpu.CompilerParams(vmem_limit_bytes=60 * 1024 * 1024),
        cost_estimate=pl.CostEstimate(
            flops=6 * slot_count * tile_edge * depth * rank_width, bytes_accessed=10_000_000, transcendentals=0
        ),
        name="contract",
    )(table, count, tile_values, third_blocks, *sources)


def combine_kernel(target_ref, received_ref, inverse_ref, out_ref, total_ref):
    slot_count, tile_edge, _ = received_ref.shape
    total_ref[...] = jnp.zeros_like(total_ref)

    def add(step, carry):
        for at in range(8):
            slot = step * 8 + at
            target = target_ref[slot]
            rows = pl.ds(pl.multiple_of(jnp.maximum(target, 0) * tile_edge, tile_edge), tile_edge)

            @pl.when(target >= 0)
            def _():
                total_ref[rows, :] += received_ref[slot]

        return carry

    lax.fori_loop(0, slot_count // 8, add, 0)
    high, low = split(total_ref[...])
    inverse_high, inverse_low = split(inverse_ref[...])
    out_ref[...] = dot32(high, inverse_high) + (dot32(low, inverse_high) + dot32(high, inverse_low))


def combine(targets, received, inverse):
    tile_edge, rank_width = received.shape[1:]
    vmem = pl.BlockSpec(memory_space=pltpu.VMEM)
    return pl.pallas_call(
        combine_kernel,
        out_shape=jax.ShapeDtypeStruct((IB_DEV * tile_edge, rank_width), jnp.float32),
        in_specs=[pl.BlockSpec(memory_space=pltpu.SMEM), vmem, vmem],
        out_specs=vmem,
        scratch_shapes=[pltpu.VMEM((IB_DEV * tile_edge, rank_width), jnp.float32)],
        compiler_params=pltpu.CompilerParams(vmem_limit_bytes=16 * 1024 * 1024),
        name="combine",
    )(targets, received, inverse)


def invert_four(s):
    det = s[0][0] * s[1][1] - s[0][1] * s[0][1]
    over = 1.0 / det
    a00, a01, a11 = s[1][1] * over, -s[0][1] * over, s[0][0] * over
    y00 = a00 * s[0][2] + a01 * s[1][2]
    y01 = a00 * s[0][3] + a01 * s[1][3]
    y10 = a01 * s[0][2] + a11 * s[1][2]
    y11 = a01 * s[0][3] + a11 * s[1][3]
    c00 = s[2][2] - (s[0][2] * y00 + s[1][2] * y10)
    c01 = s[2][3] - (s[0][2] * y01 + s[1][2] * y11)
    c11 = s[3][3] - (s[0][3] * y01 + s[1][3] * y11)
    over = 1.0 / (c00 * c11 - c01 * c01)
    d00, d01, d11 = c11 * over, -c01 * over, c00 * over
    e00 = -(y00 * d00 + y01 * d01)
    e01 = -(y00 * d01 + y01 * d11)
    e10 = -(y10 * d00 + y11 * d01)
    e11 = -(y10 * d01 + y11 * d11)
    b00 = a00 - (e00 * y00 + e01 * y01)
    b01 = a01 - (e00 * y10 + e01 * y11)
    b11 = a11 - (e10 * y10 + e11 * y11)
    return [[b00, b01, e00, e01], [b01, b11, e10, e11], [e00, e10, d00, d01], [e01, e11, d01, d11]]

def invert_block(groups):
    width = groups[0].shape[1]
    full = (8, width)
    lane = lax.broadcasted_iota(jnp.int32, full, 1)
    sub = lax.broadcasted_iota(jnp.int32, full, 0)
    for first in range(0, width, 4):
        at, off = first // 8, first % 8
        cols = [[jnp.broadcast_to(g[:, first + j : first + j + 1], full) for j in range(4)] for g in groups]
        s = [[jnp.broadcast_to(cols[at][j][off + i : off + i + 1], full) if i <= j else None for j in range(4)] for i in range(4)]
        rows = [jnp.broadcast_to(groups[at][off + i : off + i + 1], full) for i in range(4)]
        d = invert_four(s)
        new_rows = []
        for i in range(4):
            w = d[i][0] * rows[0] + d[i][1] * rows[1] + d[i][2] * rows[2] + d[i][3] * rows[3]
            for j in range(4):
                w = jnp.where(lane == first + j, d[i][j], w)
            new_rows.append(w)
        in_pivot = (lane >= first) & (lane < first + 4)
        out = []
        for k, g in enumerate(groups):
            v = jnp.where(in_pivot, 0.0, g)
            v = v - ((cols[k][0] * new_rows[0] + cols[k][1] * new_rows[1]) + (cols[k][2] * new_rows[2] + cols[k][3] * new_rows[3]))
            if k == at:
                for i in range(4):
                    v = jnp.where(sub == off + i, new_rows[i], v)
            out.append(v)
        groups = out
    return groups

def invert_kernel(block, order_ref, strips_ref, out_ref, work_ref):
    n = out_ref.shape[0]
    strip = n // strips_ref.shape[0]
    for at in range(strips_ref.shape[0]):
        work_ref[at * strip : (at + 1) * strip, :] = strips_ref[order_ref[at], 0:strip, :]
    normal = work_ref[...]
    on_diagonal = lax.broadcasted_iota(jnp.int32, (n, n), 0) == lax.broadcasted_iota(jnp.int32, (n, n), 1)
    diagonal = jnp.where(on_diagonal, normal, 0.0)
    scale_row = lax.rsqrt(jnp.sum(diagonal, axis=0, keepdims=True))
    scale_col = lax.rsqrt(jnp.sum(diagonal, axis=1, keepdims=True))
    work_ref[...] = normal * scale_col * scale_row
    for first in range(0, n, block):
        last = first + block
        groups = [work_ref[r : r + 8, first:last] for r in range(first, last, 8)]
        inner = jnp.concatenate(invert_block(groups), axis=0)
        rows = jnp.dot(inner, work_ref[first:last, :], precision=HIGHEST, preferred_element_type=jnp.float32)
        pieces = [rows[:, :first]] if first else []
        pieces.append(inner)
        if last < n:
            pieces.append(rows[:, last:])
        rows = jnp.concatenate(pieces, axis=1)
        change = jnp.dot(work_ref[:, first:last], rows, precision=HIGHEST, preferred_element_type=jnp.float32)
        lane = lax.broadcasted_iota(jnp.int32, (n, n), 1)
        work_ref[...] = jnp.where((lane >= first) & (lane < last), 0.0, work_ref[...]) - change
        work_ref[first:last, :] = rows
    out_ref[...] = work_ref[...] * scale_col * scale_row

def invert(order, strips, block=64):
    n = strips.shape[2]
    vmem = pl.BlockSpec(memory_space=pltpu.VMEM)
    return pl.pallas_call(
        functools.partial(invert_kernel, block),
        out_shape=jax.ShapeDtypeStruct((n, n), jnp.float32),
        in_specs=[pl.BlockSpec(memory_space=pltpu.SMEM), vmem],
        out_specs=vmem,
        scratch_shapes=[pltpu.VMEM((n, n), jnp.float32)],
        compiler_params=pltpu.CompilerParams(vmem_limit_bytes=16 * 1024 * 1024),
        cost_estimate=pl.CostEstimate(flops=12 * n * n * n, bytes_accessed=8 * n * n, transcendentals=0),
        name="invert",
    )(order, strips)


def local(
    tile_values,
    tile_count,
    mode1_column,
    mode1_offset,
    mode2_row,
    mode2_offset,
    mode3_offset,
    mode2_factor,
    mode3_factor,
):
    slot_count, tile_edge, _ = tile_values.shape
    rank_width = mode2_factor.shape[1]
    row_index = lax.axis_index("row")
    col_index = lax.axis_index("col")
    n_row = lax.axis_size("row")
    n_col = lax.axis_size("col")
    part = rank_width // n_col

    with jax.named_scope("gather_second"):
        n_z = n_row // 2

        def moved(array, shift):
            pairs = [(i, 2 * ((i // 2 + shift) % n_z) + i % 2) for i in range(n_row)]
            return lax.ppermute(array, "row", pairs)

        near = [1, n_z - 1, 2, n_z - 2]
        far = [3, n_z - 3, 4]
        twin = [(i, i ^ 1) for i in range(n_row)]
        up_1, down_1 = moved(mode2_factor, 1), moved(mode2_factor, -1)
        up_2, down_2 = moved(up_1, 1), moved(down_1, -1)
        up_3, down_3 = moved(up_2, 1), moved(down_2, -1)
        middle = mode2_factor.shape[0] // 2
        up_4, down_4 = moved(up_3[:middle], 1), moved(down_3[middle:], -1)
        near_own = jnp.concatenate([mode2_factor, up_1, down_1, up_2, down_2], axis=0)
        far_own = jnp.concatenate([up_3, down_3, up_4, down_4], axis=0)
        near_other = lax.ppermute(near_own, "row", twin)
        far_other = lax.ppermute(far_own, "row", twin)

    with jax.named_scope("tables"):
        slot_index = jnp.arange(slot_count, dtype=jnp.int32)
        is_live = slot_index < tile_count[0]
        chosen = (mode1_column[:, 0][None, :] == jnp.arange(n_col, dtype=jnp.int32)[:, None]) & is_live[None, :]
        chosen = chosen.astype(jnp.float32)
        earlier = (slot_index[:, None] < slot_index[None, :]).astype(jnp.float32)
        rank = jnp.dot(chosen, earlier)
        own_rank = jnp.sum(chosen * rank, axis=0).astype(jnp.int32)
        out_slot = jnp.clip(mode1_column[:, 0], 0, n_col - 1) * SLOTS + own_rank
        source = jnp.clip(mode2_row[:, 0], 0, n_row - 1)
        shift = (row_index // 2 - source // 2 + n_z) % n_z
        place_of = [0] * n_z
        for at, each in enumerate([0] + near):
            place_of[each] = at
        for at, each in enumerate(far):
            place_of[each] = at
        place = sum(jnp.where(shift == each, place_of[each], 0) for each in range(n_z))
        is_far = ((shift > 2) & (shift < n_z - 2)).astype(jnp.int32)
        is_other = (source % 2 != row_index % 2).astype(jnp.int32)
        table = jnp.stack(
            [
                place * JB_DEV + jnp.clip(mode2_offset, 0, JB_DEV - 1),
                jnp.clip(mode3_offset, 0, mode3_factor.shape[0] // tile_edge - 1),
                out_slot,
                is_far + 2 * is_other,
            ]
        ).astype(jnp.int32)
        slots = jnp.arange(SLOTS, dtype=jnp.float32)
        taken = chosen[:, None, :] * (rank[:, None, :] == slots[None, :, None])
        targets = jnp.sum(taken * (mode1_offset + 1).astype(jnp.float32), axis=2) - 1.0
        target_rows = jnp.zeros((8, rank_width), jnp.float32).at[0, : n_col * SLOTS].set(targets.reshape(-1))

    with jax.named_scope("normal"):
        strips = [gram_of(each).reshape(n_col, part, rank_width) for each in (mode2_factor, mode3_factor)]
        strips = lax.all_to_all(jnp.concatenate(strips, axis=1), "col", 0, 0)
        strips = jnp.sum(strips, axis=0)
        second_strips = lax.all_to_all(
            jnp.broadcast_to(strips[None, :part], (n_row, part, rank_width)), "row", 0, 0
        )
        normal_part = jnp.sum(second_strips, axis=0) * strips[part:]
        sent = jnp.concatenate([normal_part, target_rows], axis=0)
        side = 4

        def turned(array, along_x, along_y):
            pairs = [
                (i, (i // side + along_x) % side * side + (i % side + along_y) % side) for i in range(n_col)
            ]
            return lax.ppermute(array, "col", pairs)

        line = jnp.stack([sent] + [turned(sent, 0, shift) for shift in range(1, side)])
        spread = jnp.stack([line] + [turned(line, shift, 0) for shift in range(1, side)])
        spread = spread.reshape((n_col,) + sent.shape)
        each_col = jnp.arange(n_col, dtype=jnp.int32)
        order = (col_index // side - each_col // side + side) % side * side + (
            col_index % side - each_col % side + side
        ) % side
        order = order.astype(jnp.int32)
        received_targets = lax.dynamic_slice_in_dim(spread[:, part], col_index * SLOTS, SLOTS, 1)
        received_targets = jnp.sum(
            jnp.where(order[:, None, None] == each_col[None, :, None], received_targets[None, :, :], 0.0), axis=1
        )
        received_targets = received_targets.astype(jnp.int32).reshape(-1)

    with jax.named_scope("contract"):
        def blocks(array):
            return array.reshape(-1, tile_edge, rank_width)

        partials = contract_tiles(
            table,
            tile_count,
            tile_values,
            blocks(mode3_factor),
            [blocks(near_own), blocks(far_own), blocks(near_other), blocks(far_other)],
            n_col * SLOTS,
        )
    with jax.named_scope("exchange"):
        received = lax.all_to_all(
            partials.reshape(n_col, SLOTS * tile_edge, rank_width), "col", 0, 0
        ).reshape(n_col * SLOTS, tile_edge, rank_width)

    with jax.named_scope("inverse"):
        inverse = invert(order, spread)

    with jax.named_scope("combine"):
        return combine(received_targets, received, inverse)


def solution(mesh):
    placed = (
        P(("row", "col"), None, None),
        P(("row", "col")),
        P(("row", "col"), None),
        P(("row", "col")),
        P(("row", "col"), None),
        P(("row", "col")),
        P(("row", "col")),
        P(("row", "col"), None),
        P("col", None),
    )
    return jax.shard_map(
        local, mesh=mesh, in_specs=placed, out_specs=P(("row", "col"), None), check_vma=False
    )
```

```python
import functools

import jax
import jax.numpy as jnp
from jax import lax
from jax.experimental import pallas as pl
from jax.experimental.pallas import tpu as pltpu
from jax.sharding import PartitionSpec as P

IB_DEV = 16
JB_DEV = 8
SLOTS = 4
GROUP = 4
AHEAD = 2

HIGHEST = lax.Precision.HIGHEST


def gram_of(matrix):
    return lax.dot_general(
        matrix, matrix, (((0,), (0,)), ((), ())), precision=HIGHEST, preferred_element_type=jnp.float32
    )


def split(value):
    high = value.astype(jnp.bfloat16)
    low = (value - high.astype(jnp.float32)).astype(jnp.bfloat16)
    return high, low


def dot32(left, right):
    return jnp.dot(left, right, preferred_element_type=jnp.float32)


def contract_kernel(table_ref, count_ref, tile_hbm, third_ref, *rest):
    sources, rest = rest[:-7], rest[-7:]
    out_hbm, tile_buf, second_buf, result_buf, tile_sem, second_sem, result_sem = rest
    count = count_ref[0]
    groups = (count + GROUP - 1) // GROUP
    slot_count, tile_edge, depth = tile_hbm.shape
    chunk = min(256, depth)
    per_chunk = chunk // tile_edge

    def tile_copy(group):
        span = pl.ds(group * GROUP, GROUP)
        return pltpu.make_async_copy(tile_hbm.at[span], tile_buf.at[span], tile_sem.at[group])

    def second_copy(source, slot):
        return pltpu.make_async_copy(source.at[table_ref[0, slot]], second_buf.at[slot], second_sem.at[slot])

    def result_copy(slot):
        return pltpu.make_async_copy(result_buf.at[slot], out_hbm.at[table_ref[2, slot]], result_sem.at[slot])

    def start(group):
        tile_copy(group).start()
        for at in range(GROUP):
            slot = group * GROUP + at
            if len(sources) == 1:
                second_copy(sources[0], slot).start()
            else:
                chosen = table_ref[3, slot]
                for which, source in enumerate(sources):

                    @pl.when(chosen == which)
                    def _():
                        second_copy(source, slot).start()

    for group in range(AHEAD):

        @pl.when(group < groups)
        def _():
            start(group)

    def contract(group, carry):
        @pl.when(group + AHEAD < groups)
        def _():
            start(group + AHEAD)

        tile_copy(group).wait()
        for at in range(GROUP):
            second_copy(sources[0], group * GROUP + at).wait()
        for at in range(GROUP):
            slot = group * GROUP + at
            second = second_buf[slot]
            third = third_ref[table_ref[1, slot]]
            high, low = split(tile_buf[slot])
            both = jnp.concatenate([high, low], axis=0)
            total = jnp.zeros((2 * tile_edge, third.shape[1]), jnp.float32)
            total_low = jnp.zeros((tile_edge, third.shape[1]), jnp.float32)
            for q in range(depth // chunk):
                rows = second[q * per_chunk : (q + 1) * per_chunk]
                khatri = (rows[:, None, :] * third[None, :, :]).reshape(chunk, third.shape[1])
                khatri_high, khatri_low = split(khatri)
                total = total + dot32(both[:, q * chunk : (q + 1) * chunk], khatri_high)
                total_low = total_low + dot32(high[:, q * chunk : (q + 1) * chunk], khatri_low)
            result_buf[slot] = total[:tile_edge] + (total[tile_edge:] + total_low)
        for at in range(GROUP):
            slot = group * GROUP + at

            @pl.when(slot < count)
            def _():
                result_copy(slot).start()

        return carry

    lax.fori_loop(0, groups, contract, 0)

    def finish(slot, carry):
        result_copy(slot).wait()
        return carry

    lax.fori_loop(0, count, finish, 0)


def contract_tiles(table, count, tile_values, third_blocks, sources, out_slots):
    slot_count, tile_edge, depth = tile_values.shape
    rank_width = third_blocks.shape[2]
    smem = pl.BlockSpec(memory_space=pltpu.SMEM)
    vmem = pl.BlockSpec(memory_space=pltpu.VMEM)
    hbm = pl.BlockSpec(memory_space=pltpu.HBM)
    block = (slot_count, tile_edge, rank_width)
    return pl.pallas_call(
        contract_kernel,
        out_shape=jax.ShapeDtypeStruct((out_slots, tile_edge, rank_width), jnp.float32),
        in_specs=[smem, smem, hbm, vmem] + [hbm] * len(sources),
        out_specs=hbm,
        scratch_shapes=[
            pltpu.VMEM((slot_count, tile_edge, depth), jnp.float32),
            pltpu.VMEM(block, jnp.float32),
            pltpu.VMEM(block, jnp.float32),
            pltpu.SemaphoreType.DMA((slot_count // GROUP,)),
            pltpu.SemaphoreType.DMA((slot_count,)),
            pltpu.SemaphoreType.DMA((slot_count,)),
        ],
        compiler_params=pltpu.CompilerParams(vmem_limit_bytes=60 * 1024 * 1024),
        cost_estimate=pl.CostEstimate(
            flops=6 * slot_count * tile_edge * depth * rank_width, bytes_accessed=10_000_000, transcendentals=0
        ),
        name="contract",
    )(table, count, tile_values, third_blocks, *sources)


def combine_kernel(target_ref, received_ref, inverse_ref, out_ref, total_ref):
    slot_count, tile_edge, _ = received_ref.shape
    total_ref[...] = jnp.zeros_like(total_ref)

    def add(step, carry):
        for at in range(8):
            slot = step * 8 + at
            target = target_ref[slot]
            rows = pl.ds(pl.multiple_of(jnp.maximum(target, 0) * tile_edge, tile_edge), tile_edge)

            @pl.when(target >= 0)
            def _():
                total_ref[rows, :] += received_ref[slot]

        return carry

    lax.fori_loop(0, slot_count // 8, add, 0)
    high, low = split(total_ref[...])
    inverse_high, inverse_low = split(inverse_ref[...])
    out_ref[...] = dot32(high, inverse_high) + (dot32(low, inverse_high) + dot32(high, inverse_low))


def combine(targets, received, inverse):
    tile_edge, rank_width = received.shape[1:]
    vmem = pl.BlockSpec(memory_space=pltpu.VMEM)
    return pl.pallas_call(
        combine_kernel,
        out_shape=jax.ShapeDtypeStruct((IB_DEV * tile_edge, rank_width), jnp.float32),
        in_specs=[pl.BlockSpec(memory_space=pltpu.SMEM), vmem, vmem],
        out_specs=vmem,
        scratch_shapes=[pltpu.VMEM((IB_DEV * tile_edge, rank_width), jnp.float32)],
        compiler_params=pltpu.CompilerParams(vmem_limit_bytes=16 * 1024 * 1024),
        name="combine",
    )(targets, received, inverse)


def invert_four(s):
    det = s[0][0] * s[1][1] - s[0][1] * s[0][1]
    over = 1.0 / det
    a00, a01, a11 = s[1][1] * over, -s[0][1] * over, s[0][0] * over
    y00 = a00 * s[0][2] + a01 * s[1][2]
    y01 = a00 * s[0][3] + a01 * s[1][3]
    y10 = a01 * s[0][2] + a11 * s[1][2]
    y11 = a01 * s[0][3] + a11 * s[1][3]
    c00 = s[2][2] - (s[0][2] * y00 + s[1][2] * y10)
    c01 = s[2][3] - (s[0][2] * y01 + s[1][2] * y11)
    c11 = s[3][3] - (s[0][3] * y01 + s[1][3] * y11)
    over = 1.0 / (c00 * c11 - c01 * c01)
    d00, d01, d11 = c11 * over, -c01 * over, c00 * over
    e00 = -(y00 * d00 + y01 * d01)
    e01 = -(y00 * d01 + y01 * d11)
    e10 = -(y10 * d00 + y11 * d01)
    e11 = -(y10 * d01 + y11 * d11)
    b00 = a00 - (e00 * y00 + e01 * y01)
    b01 = a01 - (e00 * y10 + e01 * y11)
    b11 = a11 - (e10 * y10 + e11 * y11)
    return [[b00, b01, e00, e01], [b01, b11, e10, e11], [e00, e10, d00, d01], [e01, e11, d01, d11]]

def invert_block(groups):
    width = groups[0].shape[1]
    full = (8, width)
    lane = lax.broadcasted_iota(jnp.int32, full, 1)
    sub = lax.broadcasted_iota(jnp.int32, full, 0)
    for first in range(0, width, 4):
        at, off = first // 8, first % 8
        cols = [[jnp.broadcast_to(g[:, first + j : first + j + 1], full) for j in range(4)] for g in groups]
        s = [[jnp.broadcast_to(cols[at][j][off + i : off + i + 1], full) if i <= j else None for j in range(4)] for i in range(4)]
        rows = [jnp.broadcast_to(groups[at][off + i : off + i + 1], full) for i in range(4)]
        d = invert_four(s)
        new_rows = []
        for i in range(4):
            w = d[i][0] * rows[0] + d[i][1] * rows[1] + d[i][2] * rows[2] + d[i][3] * rows[3]
            for j in range(4):
                w = jnp.where(lane == first + j, d[i][j], w)
            new_rows.append(w)
        in_pivot = (lane >= first) & (lane < first + 4)
        out = []
        for k, g in enumerate(groups):
            v = jnp.where(in_pivot, 0.0, g)
            v = v - ((cols[k][0] * new_rows[0] + cols[k][1] * new_rows[1]) + (cols[k][2] * new_rows[2] + cols[k][3] * new_rows[3]))
            if k == at:
                for i in range(4):
                    v = jnp.where(sub == off + i, new_rows[i], v)
            out.append(v)
        groups = out
    return groups

def invert_kernel(block, normal_ref, out_ref, work_ref):
    n = normal_ref.shape[0]
    normal = normal_ref[...]
    on_diagonal = lax.broadcasted_iota(jnp.int32, (n, n), 0) == lax.broadcasted_iota(jnp.int32, (n, n), 1)
    diagonal = jnp.where(on_diagonal, normal, 0.0)
    scale_row = lax.rsqrt(jnp.sum(diagonal, axis=0, keepdims=True))
    scale_col = lax.rsqrt(jnp.sum(diagonal, axis=1, keepdims=True))
    work_ref[...] = normal * scale_col * scale_row
    for first in range(0, n, block):
        last = first + block
        groups = [work_ref[r : r + 8, first:last] for r in range(first, last, 8)]
        inner = jnp.concatenate(invert_block(groups), axis=0)
        rows = jnp.dot(inner, work_ref[first:last, :], precision=HIGHEST, preferred_element_type=jnp.float32)
        pieces = [rows[:, :first]] if first else []
        pieces.append(inner)
        if last < n:
            pieces.append(rows[:, last:])
        rows = jnp.concatenate(pieces, axis=1)
        change = jnp.dot(work_ref[:, first:last], rows, precision=HIGHEST, preferred_element_type=jnp.float32)
        lane = lax.broadcasted_iota(jnp.int32, (n, n), 1)
        work_ref[...] = jnp.where((lane >= first) & (lane < last), 0.0, work_ref[...]) - change
        work_ref[first:last, :] = rows
    out_ref[...] = work_ref[...] * scale_col * scale_row

def invert(normal, block=64):
    n = normal.shape[0]
    vmem = pl.BlockSpec(memory_space=pltpu.VMEM)
    return pl.pallas_call(
        functools.partial(invert_kernel, block),
        out_shape=jax.ShapeDtypeStruct((n, n), jnp.float32),
        in_specs=[vmem], out_specs=vmem,
        scratch_shapes=[pltpu.VMEM((n, n), jnp.float32)],
        compiler_params=pltpu.CompilerParams(vmem_limit_bytes=16 * 1024 * 1024),
        cost_estimate=pl.CostEstimate(flops=12 * n * n * n, bytes_accessed=8 * n * n, transcendentals=0),
        name="invert",
    )(normal)


def local(
    tile_values,
    tile_count,
    mode1_column,
    mode1_offset,
    mode2_row,
    mode2_offset,
    mode3_offset,
    mode2_factor,
    mode3_factor,
):
    slot_count, tile_edge, _ = tile_values.shape
    rank_width = mode2_factor.shape[1]
    row_index = lax.axis_index("row")
    col_index = lax.axis_index("col")
    n_row = lax.axis_size("row")
    n_col = lax.axis_size("col")
    part = rank_width // n_col

    with jax.named_scope("gather_second"):
        n_z = n_row // 2

        def moved(array, shift):
            pairs = [(i, 2 * ((i // 2 + shift) % n_z) + i % 2) for i in range(n_row)]
            return lax.ppermute(array, "row", pairs)

        near = [1, n_z - 1, 2, n_z - 2]
        far = [3, n_z - 3, 4]
        twin = [(i, i ^ 1) for i in range(n_row)]
        up_1, down_1 = moved(mode2_factor, 1), moved(mode2_factor, -1)
        up_2, down_2 = moved(up_1, 1), moved(down_1, -1)
        up_3, down_3 = moved(up_2, 1), moved(down_2, -1)
        middle = mode2_factor.shape[0] // 2
        up_4, down_4 = moved(up_3[:middle], 1), moved(down_3[middle:], -1)
        near_own = jnp.concatenate([mode2_factor, up_1, down_1, up_2, down_2], axis=0)
        near_other = lax.ppermute(near_own, "row", twin)

    with jax.named_scope("tables"):
        slot_index = jnp.arange(slot_count, dtype=jnp.int32)
        is_live = slot_index < tile_count[0]
        chosen = (mode1_column[:, 0][None, :] == jnp.arange(n_col, dtype=jnp.int32)[:, None]) & is_live[None, :]
        chosen = chosen.astype(jnp.float32)
        earlier = (slot_index[:, None] < slot_index[None, :]).astype(jnp.float32)
        rank = jnp.dot(chosen, earlier)
        own_rank = jnp.sum(chosen * rank, axis=0).astype(jnp.int32)
        out_slot = jnp.clip(mode1_column[:, 0], 0, n_col - 1) * SLOTS + own_rank
        source = jnp.clip(mode2_row[:, 0], 0, n_row - 1)
        shift = (row_index // 2 - source // 2 + n_z) % n_z
        place_of = [0] * n_z
        for at, each in enumerate([0] + near):
            place_of[each] = at
        for at, each in enumerate(far):
            place_of[each] = at
        place = sum(jnp.where(shift == each, place_of[each], 0) for each in range(n_z))
        is_far = ((shift > 2) & (shift < n_z - 2)).astype(jnp.int32)
        is_other = (source % 2 != row_index % 2).astype(jnp.int32)
        table = jnp.stack(
            [
                place * JB_DEV + jnp.clip(mode2_offset, 0, JB_DEV - 1),
                jnp.clip(mode3_offset, 0, mode3_factor.shape[0] // tile_edge - 1),
                out_slot,
                is_far + 2 * is_other,
            ]
        ).astype(jnp.int32)
        held_up_3, near_other, table = lax.optimization_barrier((up_3, near_other, table))
        far_own = jnp.concatenate([held_up_3, down_3, up_4, down_4], axis=0)
        far_other = lax.ppermute(far_own, "row", twin)
        slots = jnp.arange(SLOTS, dtype=jnp.float32)
        taken = chosen[:, None, :] * (rank[:, None, :] == slots[None, :, None])
        targets = jnp.sum(taken * (mode1_offset + 1).astype(jnp.float32), axis=2) - 1.0
        target_rows = jnp.zeros((8, rank_width), jnp.float32).at[0, : n_col * SLOTS].set(targets.reshape(-1))

    with jax.named_scope("normal"):
        strips = [gram_of(each).reshape(n_col, part, rank_width) for each in (mode2_factor, mode3_factor)]
        strips = lax.all_to_all(jnp.concatenate(strips, axis=1), "col", 0, 0)
        strips = jnp.sum(strips, axis=0)
        second_strips = lax.all_to_all(
            jnp.broadcast_to(strips[None, :part], (n_row, part, rank_width)), "row", 0, 0
        )
        normal_part = jnp.sum(second_strips, axis=0) * strips[part:]
        sent = jnp.concatenate([normal_part, target_rows], axis=0)
        spread = lax.all_to_all(jnp.broadcast_to(sent[None], (n_col,) + sent.shape), "col", 0, 0)
        normal_matrix = spread[:, :part].reshape(rank_width, rank_width)
        received_targets = lax.dynamic_slice_in_dim(spread[:, part], col_index * SLOTS, SLOTS, 1)
        received_targets = received_targets.astype(jnp.int32).reshape(-1)

    with jax.named_scope("contract"):
        def blocks(array):
            return array.reshape(-1, tile_edge, rank_width)

        partials = contract_tiles(
            table,
            tile_count,
            tile_values,
            blocks(mode3_factor),
            [blocks(near_own), blocks(far_own), blocks(near_other), blocks(far_other)],
            n_col * SLOTS,
        )
    with jax.named_scope("exchange"):
        received = lax.all_to_all(
            partials.reshape(n_col, SLOTS * tile_edge, rank_width), "col", 0, 0
        ).reshape(n_col * SLOTS, tile_edge, rank_width)

    with jax.named_scope("inverse"):
        inverse = invert(normal_matrix)

    with jax.named_scope("combine"):
        return combine(received_targets, received, inverse)


def solution(mesh):
    placed = (
        P(("row", "col"), None, None),
        P(("row", "col")),
        P(("row", "col"), None),
        P(("row", "col")),
        P(("row", "col"), None),
        P(("row", "col")),
        P(("row", "col")),
        P(("row", "col"), None),
        P("col", None),
    )
    return jax.shard_map(
        local, mesh=mesh, in_specs=placed, out_specs=P(("row", "col"), None), check_vma=False
    )
```
